32 devices in a mesh: grp: 4 (over y, core), dom: 8 (over z, x).
Axes of the slice: x: 2, y: 2, z: 4, core: 2. Of those that a mesh axis runs over, the one named last changes fastest.
Arguments:
- entity: bfloat16 [65536, 256], P(('grp', 'dom')), may hold values from -1.5 to 1.5
- entity_acc: float32 [65536], P(('grp', 'dom')), may hold values from 0.1 to 1
- relation: float32 [1000, 256], replicated, may hold values from -3 to 3
- rel_acc: float32 [1000], replicated, may hold values from 0.1 to 1
- edge_src: int32 [32, 2, 3072], P(('grp', 'dom')), may hold values from 0 to 2047
- edge_rel: int32 [32, 2, 3072], P(('grp', 'dom')), may hold values from 0 to 999
- edge_dst: int32 [32, 2, 3072], P(('grp', 'dom')), may hold values from 0 to 2047
- negatives: int32 [32, 2, 6, 512], P(('grp', 'dom')), may hold values from 0 to 2047
Outputs:
- entity_new: bfloat16 [65536, 256], P(('grp', 'dom'))
- entity_acc_new: float32 [65536], P(('grp', 'dom'))
- relation_new: float32 [1000, 256], replicated
- rel_acc_new: float32 [1000], replicated
The draws below stay inside these ranges and needn't reach their ends.
All inputs are finite; a program needn't handle non-finite values.
Results may differ from the reference program's by a relative error of at most 0.0042.
Values may be sent and summed in bfloat16 or wider, within the bound.
No kernel may reach another device: no remote copies, remote signals or barrier semaphores. Data moves between devices by JAX's collectives and lax.ppermute only.
A program may use at most 128 MiB of HBM per device.

```python
import math
import jax
import jax.numpy as jnp
import numpy as np
from jax import lax

DIM = 256
NREL = 1000
NEG = 512
ROWS = 2048
EDGES = 3072
SPANS = 6
PARTS_SIZE = 32
N_GRP = 4
N_DOM = 8


def draw_entity(key, part):
    total_rows = N_GRP * N_DOM * ROWS
    full_shape = (total_rows, DIM)
    values = jnp.clip(0.3 * jax.random.normal(key, full_shape), -1.2, 1.2)
    return values.astype(jnp.bfloat16)


def draw_relation(key, part):
    values = jnp.clip(jax.random.normal(key, (NREL, DIM)), -3.0, 3.0)
    return values.astype(jnp.float32)


def with_ends(values, stream_key, low, high):
    place = [jax.random.randint(jax.random.fold_in(stream_key, axis), (), 0, length) for axis, length in enumerate(values.shape)]
    widest = values.shape.index(max(values.shape))
    neighbour = place[:widest] + [(place[widest] + 1) % values.shape[widest]] + place[widest + 1:]
    return values.at[tuple(place)].set(low).at[tuple(neighbour)].set(high)


def block_levels(key, dims, shards, smallest, largest):
    def one(position, parts):
        draws = jax.random.uniform(jax.random.fold_in(jax.random.fold_in(key, 6), position), (parts,), jnp.float32, smallest / len(shards), largest / len(shards))
        return jnp.repeat(jnp.exp(draws), dims[position] // parts).reshape((-1,) + (1,) * (len(dims) - position - 1))

    level = one(*shards[0])
    for cut in shards[1:]:
        level = level * one(*cut)
    return level


def rank_table(number_of, lean):
    loads = [(1 << 20) // math.isqrt(rank ** lean) + 1 for rank in range(1, number_of + 1)]
    width = 1 + sum(loads) // (1 << 30)
    return np.cumsum(np.array([max(1, weight // width) for weight in loads]))


def skewed_ids(rng, shape, number_of, lean):
    grid = rank_table(number_of, lean)
    pick = jax.random.randint(jax.random.fold_in(rng, 1), shape, 0, int(grid[number_of - 1]))
    rank = jnp.searchsorted(jnp.asarray(grid, jnp.int32), pick, side="right")
    return jax.random.permutation(jax.random.fold_in(rng, 2), number_of)[rank].astype(jnp.int32)


def setup_inputs(seed: int = 0) -> dict:
    seeds = jax.random.split(jax.random.key(seed), 9)
    return {
        "entity": draw_entity(jax.random.fold_in(seeds[8], 71), 0),
        "entity_acc": jnp.clip(jnp.exp(math.log(1.0) - 2.3025851 * jax.random.uniform(seeds[1], (PARTS_SIZE * ROWS,), jnp.float32) ** block_levels(seeds[1], (PARTS_SIZE * ROWS,), ((0, 32),), -0.2, 0.2)), 0.1, 1.0),
        "relation": draw_relation(jax.random.fold_in(seeds[8], 71), 0),
        "rel_acc": jnp.clip(jnp.exp(jax.random.uniform(seeds[3], (NREL,), jnp.float32, math.log(0.1), math.log(1.0))), 0.1, 1.0),
        "edge_src": with_ends(jax.random.randint(seeds[4], (PARTS_SIZE, 2, EDGES), 0, ROWS), jax.random.fold_in(seeds[4], 1), 0, ROWS - 1).astype(jnp.int32),
        "edge_rel": with_ends(skewed_ids(seeds[5], (PARTS_SIZE, 2, EDGES), NREL, 2), jax.random.fold_in(seeds[5], 3), 0, NREL - 1).astype(jnp.int32),
        "edge_dst": with_ends(jax.random.randint(seeds[6], (PARTS_SIZE, 2, EDGES), 0, ROWS), jax.random.fold_in(seeds[6], 1), 0, ROWS - 1).astype(jnp.int32),
        "negatives": with_ends(jax.random.randint(seeds[7], (PARTS_SIZE, 2, SPANS, NEG), 0, ROWS), jax.random.fold_in(seeds[7], 1), 0, ROWS - 1).astype(jnp.int32),
    }


learn_rate = 0.3

def bucket(left_block, right_block, relation, source_rows, rel_ids, target_rows, neg_rows):
    middle = left_block.shape[1] // 2
    features = left_block.shape[1]
    heads = jnp.take(left_block, source_rows, axis=0).astype(jnp.float32)
    rel_rows = jnp.take(relation, rel_ids, axis=0)
    head_real, head_imag = (heads[:, :middle], heads[:, middle:])
    rel_real, rel_imag = (rel_rows[:, :middle], rel_rows[:, middle:])
    query = jnp.concatenate([head_real * rel_real - head_imag * rel_imag, head_real * rel_imag + head_imag * rel_real], axis=1).astype(jnp.bfloat16)
    targets = jnp.take(right_block, target_rows, axis=0)
    spans = neg_rows.shape[0]
    query_blocks = query.reshape(spans, -1, features)
    target_blocks = targets.reshape(spans, -1, features)

    def one_span(pieces):
        queries, tail_rows, cand_ids = pieces
        cands = jnp.take(right_block, cand_ids, axis=0)
        positive = lax.optimization_barrier(jnp.sum(queries.astype(jnp.float32) * tail_rows.astype(jnp.float32), axis=1))
        scores = lax.dot_general(queries, cands, (((1,), (1,)), ((), ())), preferred_element_type=jnp.float32)
        peak_score = jnp.maximum(lax.optimization_barrier(jnp.max(scores, axis=1)), positive)
        expd = jnp.exp(scores - peak_score[:, None])
        own_term = jnp.exp(positive - peak_score)
        denominator = own_term + lax.optimization_barrier(jnp.sum(expd, axis=1))
        shares = (expd / denominator[:, None]).astype(jnp.bfloat16)
        coefficient = own_term / denominator - 1.0
        d_query = coefficient[:, None] * tail_rows.astype(jnp.float32) + jnp.dot(shares, cands, preferred_element_type=jnp.float32)
        d_cands = lax.dot_general(shares, queries, (((0,), (0,)), ((), ())), preferred_element_type=jnp.float32)
        d_tails = coefficient[:, None] * queries.astype(jnp.float32)
        return (d_query, d_cands, d_tails)
    d_query, d_cands, d_tails = lax.map(one_span, (query_blocks, target_blocks, neg_rows))
    d_query = d_query.reshape(-1, features)
    d_right = jnp.zeros(right_block.shape, jnp.float32).at[target_rows].add(d_tails.reshape(-1, features))
    d_right = d_right.at[neg_rows.reshape(-1)].add(d_cands.reshape(-1, features))
    grad_real, grad_imag = (d_query[:, :middle], d_query[:, middle:])
    d_heads = jnp.concatenate([grad_real * rel_real + grad_imag * rel_imag, grad_imag * rel_real - grad_real * rel_imag], axis=1)
    d_rels = jnp.concatenate([grad_real * head_real + grad_imag * head_imag, grad_imag * head_real - grad_real * head_imag], axis=1)
    d_left = jnp.zeros(left_block.shape, jnp.float32).at[source_rows].add(d_heads)
    d_rel = jnp.zeros(relation.shape, jnp.float32).at[rel_ids].add(d_rels)
    return (d_left, d_right, d_rel)

def reference(entity, entity_acc, relation, rel_acc, edge_src, edge_rel, edge_dst, negatives):
    features = entity.shape[1]
    blocks = entity.reshape(N_GRP, N_DOM, ROWS, features)
    inner_block = jnp.roll(blocks, N_DOM // 2, axis=1).reshape(-1, ROWS, features)
    outer_block = jnp.roll(blocks, 1, axis=0).reshape(-1, ROWS, features)
    own_blocks = blocks.reshape(-1, ROWS, features)

    def per_partition(rel_sum, pieces):
        left_block, first_right, second_right, source_rows, rel_ids, target_rows, neg_rows = pieces
        left_one, right_one, rels_one = bucket(left_block, first_right, relation, source_rows[0], rel_ids[0], target_rows[0], neg_rows[0])
        left_two, right_two, rels_two = bucket(left_block, second_right, relation, source_rows[1], rel_ids[1], target_rows[1], neg_rows[1])
        return (rel_sum + (rels_one + rels_two), (left_one + left_two, right_one.astype(jnp.bfloat16), right_two.astype(jnp.bfloat16)))
    rel_grad, outputs = lax.scan(per_partition, jnp.zeros(relation.shape, jnp.float32), (own_blocks, inner_block, outer_block, edge_src, edge_rel, edge_dst, negatives))
    own_grad, inner_grad, outer_grad = outputs
    back_inner = jnp.roll(inner_grad.reshape(N_GRP, N_DOM, ROWS, features), N_DOM // 2, axis=1).reshape(-1, features)
    back_outer = jnp.roll(outer_grad.reshape(N_GRP, N_DOM, ROWS, features), -1, axis=0).reshape(-1, features)
    row_grad = own_grad.reshape(-1, features) + back_inner.astype(jnp.float32) + back_outer.astype(jnp.float32)
    entity_acc_new = entity_acc + lax.optimization_barrier(jnp.mean(row_grad * row_grad, axis=1))
    entity_new = (entity.astype(jnp.float32) - learn_rate * row_grad / jnp.sqrt(entity_acc_new)[:, None]).astype(jnp.bfloat16)
    rel_acc_new = rel_acc + lax.optimization_barrier(jnp.mean(rel_grad * rel_grad, axis=1))
    relation_new = relation - learn_rate * rel_grad / jnp.sqrt(rel_acc_new)[:, None]
    return (entity_new, entity_acc_new, relation_new, rel_acc_new)
```

```python
import jax
import jax.numpy as jnp
from jax import lax
from jax.experimental import pallas as pl
from jax.experimental.pallas import tpu as pltpu
from jax.sharding import PartitionSpec as P

learn_rate = 0.3
bf16 = jnp.bfloat16
f32 = jnp.float32


def passed_along(block, axis, distance):
    devices = range(lax.axis_size(axis))
    route = [((i - distance) % len(devices), i) for i in devices]
    return lax.ppermute(block, axis, route)


def dot_nn(a, b):
    return jnp.dot(a, b, preferred_element_type=f32)


def dot_nt(a, b):
    return lax.dot_general(a, b, (((1,), (1,)), ((), ())), preferred_element_type=f32)


def one_hot(ids, rows):
    shape = (rows, ids.shape[1])
    match = ids.astype(jnp.int16) == lax.broadcasted_iota(jnp.int16, shape, 0)
    return jnp.where(match, jnp.ones((), bf16), jnp.zeros((), bf16))


def bucket_kernel(ids_ref, left_ref, right_ref, rel_ref, rel_in_ref, d_left_ref, d_right_ref, d_rel_ref, right_sum):
    step = pl.program_id(0)
    features, rows = left_ref.shape
    middle = features // 2
    n_rel = rel_ref.shape[1]

    @pl.when(step == 0)
    def _():
        d_left_ref[...] = jnp.zeros_like(d_left_ref)
        d_rel_ref[...] = rel_in_ref[...]
        right_sum[...] = jnp.zeros_like(right_sum)

    ids = ids_ref[0]
    pick_source = one_hot(ids[0:1], rows)
    heads = dot_nn(left_ref[...], pick_source)
    pick_rel = one_hot(ids[1:2], n_rel)
    both = dot_nn(rel_ref[...], pick_rel)
    rel = both[:features] + both[features:]
    h_re, h_im = heads[:middle], heads[middle:]
    r_re, r_im = rel[:middle], rel[middle:]
    query = jnp.concatenate([h_re * r_re - h_im * r_im, h_re * r_im + h_im * r_re], 0).astype(bf16)

    pick_target = one_hot(ids[2:3], rows)
    tails = dot_nn(right_ref[...], pick_target)
    pick_neg = one_hot(ids[3:4], rows)
    cands = dot_nn(right_ref[...], pick_neg).astype(bf16)

    query32 = query.astype(f32)
    positive = jnp.sum(query32 * tails, axis=0, keepdims=True)
    scores = dot_nn(cands.T, query)
    peak = jnp.maximum(jnp.max(scores, axis=0, keepdims=True), positive)
    expd = jnp.exp(scores - peak)
    own = jnp.exp(positive - peak)
    inverse = 1.0 / (own + jnp.sum(expd, axis=0, keepdims=True))
    shares = (expd * inverse).astype(bf16)
    coefficient = own * inverse - 1.0

    d_cands = dot_nt(query, shares).astype(bf16)
    d_tails = (coefficient * query32).astype(bf16)
    right_sum[...] += dot_nt(pick_target, d_tails) + dot_nt(pick_neg, d_cands)

    grad = coefficient * tails + dot_nn(cands, shares)
    g_re, g_im = grad[:middle], grad[middle:]
    d_heads = jnp.concatenate([g_re * r_re + g_im * r_im, g_im * r_re - g_re * r_im], 0).astype(bf16)
    d_left_ref[...] += dot_nt(pick_source, d_heads)
    d_rels = jnp.concatenate([g_re * h_re + g_im * h_im, g_im * h_re - g_re * h_im], 0).astype(bf16)
    d_rel_ref[...] += dot_nt(pick_rel, d_rels)

    @pl.when(step == pl.num_programs(0) - 1)
    def _():
        d_right_ref[...] = right_sum[...].astype(bf16)


def bucket(ids, left, right, rel, rel_sum):
    spans, _, span = ids.shape
    features, rows = left.shape
    n_rel = rel.shape[1]

    def whole(shape):
        return pl.BlockSpec(shape, lambda s: (0,) * len(shape))

    return pl.pallas_call(
        bucket_kernel,
        grid=(spans,),
        in_specs=[
            pl.BlockSpec((1, 4, span), lambda s: (s, 0, 0)),
            whole((features, rows)),
            whole((features, rows)),
            whole((2 * features, n_rel)),
            whole((n_rel, features)),
        ],
        out_specs=[whole((rows, features)), whole((rows, features)), whole((n_rel, features))],
        out_shape=[
            jax.ShapeDtypeStruct((rows, features), f32),
            jax.ShapeDtypeStruct((rows, features), bf16),
            jax.ShapeDtypeStruct((n_rel, features), f32),
        ],
        scratch_shapes=[pltpu.VMEM((rows, features), f32)],
        compiler_params=pltpu.CompilerParams(
            dimension_semantics=("arbitrary",), vmem_limit_bytes=52 << 20
        ),
        cost_estimate=pl.CostEstimate(
            flops=2 * spans * span * features * (6 * rows + 3 * n_rel + 3 * span),
            bytes_accessed=14 << 20,
            transcendentals=spans * span * span,
        ),
        name="bucket",
    )(ids, left, right, rel, rel_sum)


def relation_total(partial, axes):
    devices = 1
    for axis in axes:
        devices *= lax.axis_size(axis)
    rows, features = partial.shape
    blocks = partial.astype(bf16).reshape(devices, rows // devices, features)
    mine = lax.all_to_all(blocks, axes, 0, 0, tiled=True)
    mine = jnp.sum(mine.astype(f32), axis=0).astype(bf16)
    spread = jnp.broadcast_to(mine[None], blocks.shape)
    return lax.all_to_all(spread, axes, 0, 0, tiled=True).reshape(rows, features).astype(f32)


def body(entity, entity_acc, relation, rel_acc, edge_src, edge_rel, edge_dst, negatives):
    axes = ("grp", "dom")
    half_group = lax.axis_size("dom") // 2
    n_rel, features = relation.shape
    spans, span = negatives.shape[2:]
    devices = lax.axis_size("grp") * lax.axis_size("dom")
    rel_rows = -(-n_rel // max(128, 8 * devices)) * max(128, 8 * devices)

    own = entity.T
    inner_block = passed_along(own, "dom", half_group)
    outer_block = passed_along(own, "grp", 1)
    padded = jnp.pad(relation, ((0, rel_rows - n_rel), (0, 0))).T
    rel_high = padded.astype(bf16)
    rel_low = (padded - rel_high.astype(f32)).astype(bf16)
    rel = jnp.concatenate([rel_high, rel_low], axis=0)
    ids = jnp.stack(
        [a[0].reshape(2, spans, span) for a in (edge_src, edge_rel, edge_dst, negatives)], axis=2
    )

    left_two, right_two, rel_sum = bucket(
        ids[1], own, outer_block, rel, jnp.zeros((rel_rows, features), f32)
    )
    back_outer = passed_along(right_two, "grp", -1)
    left_one, right_one, rel_sum = bucket(ids[0], own, inner_block, rel, rel_sum)
    back_inner = passed_along(right_one, "dom", half_group)
    row_grad = left_one + left_two + back_inner.astype(f32) + back_outer.astype(f32)
    entity_acc_new = entity_acc + jnp.mean(row_grad * row_grad, axis=1)
    entity_new = (
        entity.astype(f32) - learn_rate * row_grad / jnp.sqrt(entity_acc_new)[:, None]
    ).astype(bf16)
    rel_total = relation_total(rel_sum, axes)[:n_rel]
    rel_acc_new = rel_acc + jnp.mean(rel_total * rel_total, axis=1)
    relation_new = relation - learn_rate * rel_total / jnp.sqrt(rel_acc_new)[:, None]
    return (entity_new, entity_acc_new, relation_new, rel_acc_new)


def solution(mesh):
    return jax.shard_map(
        body,
        mesh=mesh,
        in_specs=(
            P(("grp", "dom"), None),
            P(("grp", "dom")),
            P(),
            P(),
            P(("grp", "dom"), None, None),
            P(("grp", "dom"), None, None),
            P(("grp", "dom"), None, None),
            P(("grp", "dom"), None, None, None),
        ),
        out_specs=(P(("grp", "dom"), None), P(("grp", "dom")), P(), P()),
        check_vma=False,
    )
```

```python
import jax
import jax.numpy as jnp
from jax import lax
from jax.experimental import pallas as pl
from jax.experimental.pallas import tpu as pltpu
from jax.sharding import PartitionSpec as P

learn_rate = 0.3
bf16 = jnp.bfloat16
f32 = jnp.float32
VMEM_LIMIT = 52 << 20


def dot_nn(a, b):
    return jnp.dot(a, b, preferred_element_type=f32)


def dot_nt(a, b):
    return lax.dot_general(a, b, (((1,), (1,)), ((), ())), preferred_element_type=f32)


def one_hot(ids, rows, first=0):
    shape = (rows, ids.shape[1])
    match = (ids - first).astype(jnp.int16) == lax.broadcasted_iota(jnp.int16, shape, 0)
    return jnp.where(match, jnp.ones((), bf16), jnp.zeros((), bf16))


def whole(shape):
    return pl.BlockSpec(shape, lambda s: (0,) * len(shape))


def across(height, width):
    return pl.BlockSpec((height, width), lambda s: (0, s))


def params():
    return pltpu.CompilerParams(dimension_semantics=("arbitrary",), vmem_limit_bytes=VMEM_LIMIT)


def halves(a):
    middle = a.shape[0] // 2
    return a[:middle], a[middle:]


def make_query(source, rel_ids, left, rel_table):
    features, rows = left.shape
    heads = dot_nn(left, one_hot(source, rows))
    both = dot_nn(rel_table, one_hot(rel_ids, rel_table.shape[1]))
    rel = both[:features] + both[features:]
    h_re, h_im = halves(heads)
    r_re, r_im = halves(rel)
    query = jnp.concatenate([h_re * r_re - h_im * r_im, h_re * r_im + h_im * r_re], 0)
    return heads, rel, query.astype(bf16)


def make_gradients(targets, negatives, heads, rel, query, right, heads_out, tails_out, cands_out, rels_out):
    rows = right.shape[1]
    tails = dot_nn(right, one_hot(targets, rows))
    cands = dot_nn(right, one_hot(negatives, rows)).astype(bf16)
    query32 = query.astype(f32)
    positive = jnp.sum(query32 * tails, axis=0, keepdims=True)
    scores = dot_nn(cands.T, query)
    peak = jnp.maximum(jnp.max(scores, axis=0, keepdims=True), positive)
    expd = jnp.exp(scores - peak)
    own = jnp.exp(positive - peak)
    inverse = 1.0 / (own + jnp.sum(expd, axis=0, keepdims=True))
    shares = (expd * inverse).astype(bf16)
    coefficient = own * inverse - 1.0
    tails_out[...] = (coefficient * query32).astype(bf16)
    cands_out[...] = dot_nt(query, shares).astype(bf16)
    grad = coefficient * tails + dot_nn(cands, shares)
    g_re, g_im = halves(grad)
    r_re, r_im = halves(rel)
    h_re, h_im = halves(heads)
    heads_out[...] = jnp.concatenate(
        [g_re * r_re + g_im * r_im, g_im * r_re - g_re * r_im], 0
    ).astype(bf16)
    rels_out[...] = jnp.concatenate(
        [g_re * h_re + g_im * h_im, g_im * h_re - g_re * h_im], 0
    ).astype(bf16)


def query_kernel(ids_ref, left_ref, table_ref, heads_ref, rel_ref, query_ref):
    ids = ids_ref[...]
    heads, rel, query = make_query(ids[0:1], ids[1:2], left_ref[...], table_ref[...])
    heads_ref[...] = heads.astype(bf16)
    rel_ref[...] = rel
    query_ref[...] = query


def gradient_kernel(ids_ref, heads_ref, rel_ref, query_ref, right_ref, *outs):
    ids = ids_ref[...]
    heads = heads_ref[...].astype(f32)
    make_gradients(ids[2:3], ids[3:4], heads, rel_ref[...], query_ref[...], right_ref[...], *outs)


def paired_kernel(home_ref, ids_ref, own_ref, met_ref, passed_ref, table_ref, *rest):
    *outs, left = rest

    @pl.when(pl.program_id(0) == 0)
    def _():
        @pl.when(home_ref[0] == 1)
        def _():
            left[...] = own_ref[...]

        @pl.when(home_ref[0] == 0)
        def _():
            left[...] = passed_ref[...]

    ids = ids_ref[...]
    heads, rel, query = make_query(ids[0:1], ids[1:2], left[...], table_ref[...])
    make_gradients(ids[2:3], ids[3:4], heads, rel, query, met_ref[...], *outs)


def gradient_shapes(features, edges):
    return [jax.ShapeDtypeStruct((features, edges), bf16)] * 4


def gradient_specs(features, span):
    return [across(features, span)] * 4


def cost(units, span, features, rows):
    return pl.CostEstimate(flops=units * span, bytes_accessed=1 << 16, transcendentals=0)


def query_call(ids, left, table, span):
    edges = ids.shape[1]
    features, rows = left.shape
    return pl.pallas_call(
        query_kernel,
        grid=(edges // span,),
        in_specs=[across(4, span), whole(left.shape), whole(table.shape)],
        out_specs=[across(features, span)] * 3,
        out_shape=[
            jax.ShapeDtypeStruct((features, edges), bf16),
            jax.ShapeDtypeStruct((features, edges), f32),
            jax.ShapeDtypeStruct((features, edges), bf16),
        ],
        compiler_params=params(),
        cost_estimate=cost(2, edges, features, rows),
        name="queries",
    )(ids, left, table)


def gradient_call(ids, heads, rel, query, right, span):
    features, edges = heads.shape
    return pl.pallas_call(
        gradient_kernel,
        grid=(edges // span,),
        in_specs=[across(4, span)] + [across(features, span)] * 3 + [whole(right.shape)],
        out_specs=gradient_specs(features, span),
        out_shape=gradient_shapes(features, edges),
        compiler_params=params(),
        cost_estimate=cost(3, edges, features, right.shape[1]),
        name="gradients",
    )(ids, heads, rel, query, right)


def paired_call(home, ids, own, met, passed, table, span):
    edges = ids.shape[1]
    features, rows = own.shape
    return pl.pallas_call(
        paired_kernel,
        grid=(edges // span,),
        in_specs=[pl.BlockSpec(memory_space=pltpu.SMEM), across(4, span)]
        + [whole(own.shape)] * 3
        + [whole(table.shape)],
        out_specs=gradient_specs(features, span),
        out_shape=gradient_shapes(features, edges),
        scratch_shapes=[pltpu.VMEM(own.shape, bf16)],
        compiler_params=params(),
        cost_estimate=cost(5, edges, features, rows),
        name="paired",
    )(home, ids, own, met, passed, table)


def scatter_kernel(chunk, lines, has_start, *refs):
    first = pl.program_id(0) * chunk
    n_pairs = len(lines)
    ins = 2 * n_pairs + has_start
    total = None
    for k, line in enumerate(lines):
        part = dot_nt(one_hot(refs[2 * k][line : line + 1, :], chunk, first), refs[2 * k + 1][...])
        total = part if total is None else total + part
    if has_start:
        total = total + refs[2 * n_pairs][...].astype(f32)
    for out_ref in refs[ins:]:
        out_ref[...] = total.astype(out_ref.dtype)


def scatter_call(pairs, rows, dtypes, start=None, chunk=512):
    features = pairs[0][2].shape[0]
    chunk = min(chunk, rows)
    operands, specs = [], []
    for ids, _, vectors in pairs:
        operands += [ids, vectors]
        specs += [whole(ids.shape), whole(vectors.shape)]
    down = pl.BlockSpec((chunk, features), lambda s: (s, 0))
    if start is not None:
        operands.append(start)
        specs.append(down)

    def kernel(*refs):
        scatter_kernel(chunk, [line for _, line, _ in pairs], start is not None, *refs)

    outs = pl.pallas_call(
        kernel,
        grid=(rows // chunk,),
        in_specs=specs,
        out_specs=[down] * len(dtypes),
        out_shape=[jax.ShapeDtypeStruct((rows, features), dtype) for dtype in dtypes],
        compiler_params=params(),
        cost_estimate=cost(1, sum(v.shape[1] for _, _, v in pairs), features, rows),
        name="scatter",
    )(*operands)
    return outs[0] if len(outs) == 1 else outs


def update_kernel(home_ref, entity_ref, acc_ref, left_ref, outer_ref, inner_ref, back_ref, new_ref, acc_new_ref):
    rows = entity_ref.shape[0]
    grad = left_ref[...] + outer_ref[...].astype(f32) + back_ref[...].astype(f32)
    grad = grad + jnp.where(home_ref[0] == 1, inner_ref[...].astype(f32), 0.0)
    mean = jnp.mean(grad * grad, axis=1, keepdims=True)
    acc_new = acc_ref[...] + jnp.broadcast_to(mean, (rows, 128)).T[:1]
    acc_new_ref[...] = acc_new
    scale = learn_rate / jnp.sqrt(jnp.broadcast_to(acc_new, (128, rows)).T[:, :1])
    new_ref[...] = (entity_ref[...].astype(f32) - scale * grad).astype(bf16)


def update_call(home, entity, acc, left, outer, inner, back, chunk=512):
    rows, features = entity.shape
    down = pl.BlockSpec((chunk, features), lambda s: (s, 0))
    line = pl.BlockSpec((1, chunk), lambda s: (0, s))
    new, acc_new = pl.pallas_call(
        update_kernel,
        grid=(rows // chunk,),
        in_specs=[pl.BlockSpec(memory_space=pltpu.SMEM), down, line, down, down, down, down],
        out_specs=[down, line],
        out_shape=[jax.ShapeDtypeStruct((rows, features), bf16), jax.ShapeDtypeStruct((1, rows), f32)],
        compiler_params=params(),
        cost_estimate=pl.CostEstimate(flops=10 * rows * features, bytes_accessed=10 << 20, transcendentals=rows),
        name="update",
    )(home, entity, acc.reshape(1, rows), left, outer, inner, back)
    return new, acc_new.reshape(rows)


def relation_mine(partial, axes):
    devices = 1
    for axis in axes:
        devices *= lax.axis_size(axis)
    rows, features = partial.shape
    return lax.all_to_all(partial.reshape(devices, rows // devices, features), axes, 0, 0, tiled=True)


def relation_spread(pieces, axes):
    mine = jnp.sum(pieces.astype(f32), axis=0).astype(bf16)
    spread = jnp.broadcast_to(mine[None], pieces.shape)
    return lax.all_to_all(spread, axes, 0, 0, tiled=True).reshape(-1, pieces.shape[2]).astype(f32)


def body(entity, entity_acc, relation, rel_acc, edge_src, edge_rel, edge_dst, negatives):
    axes = ("grp", "dom")
    groups, doms = lax.axis_size("grp"), lax.axis_size("dom")
    half = doms // 2
    rows, features = entity.shape
    n_rel = relation.shape[0]
    spans, span = negatives.shape[2:]
    edges = spans * span
    step = max(128, 8 * groups * doms)
    rel_rows = -(-n_rel // step) * step

    places = [(g, d) for g in range(groups) for d in range(doms)]

    def is_home(g, d):
        return g % 2 == d // half

    def send(block, to, only=lambda g, d: True):
        route = []
        for g, d in places:
            if only(g, d):
                h, e = to(g, d)
                route.append((g * doms + d, h % groups * doms + e % doms))
        return lax.ppermute(block, axes, route)

    def guest(g, d):
        return not is_home(g, d)

    def meeting(g, d):
        return (g ^ 1, d) if is_home(g, d) else (g, d + half)

    def parting(g, d):
        return (g, d + half) if is_home(g, d) else (g ^ 1, d)

    def neighbour(g, d):
        return g ^ 1, d

    home = (lax.axis_index("grp") % 2 == lax.axis_index("dom") // half).astype(jnp.int32).reshape(1)

    def id_lines(bucket):
        lines = [a[0, bucket].reshape(edges) for a in (edge_src, edge_rel, edge_dst, negatives)]
        return jnp.stack(lines)

    own = entity.T
    met = send(own, meeting)
    outer = send(own, lambda g, d: (g + 1, d))
    ids_two, ids_one = id_lines(1), id_lines(0)
    sent_ids = send(ids_one, lambda g, d: (g ^ 1, d + half), guest)
    ids_one = jnp.where(home == 1, ids_one, sent_ids)

    padded = jnp.pad(relation, ((0, rel_rows - n_rel), (0, 0))).T
    high = lax.reduce_precision(padded, 8, 7)
    table = jnp.concatenate([high.astype(bf16), (padded - high).astype(bf16)], axis=0)

    heads, rel, query = query_call(ids_two, own, table, span)
    dl_two, dt_two, dc_two, dp_two = gradient_call(ids_two, heads, rel, query, outer, span)
    met, dp_two = lax.optimization_barrier((met, dp_two))
    passed = send(met, neighbour, is_home)
    rel_part = scatter_call([(ids_two, 1, dp_two)], rel_rows, [f32])
    passed, rel_part = lax.optimization_barrier((passed, rel_part))
    dl_one, dt_one, dc_one, dp_one = paired_call(home, ids_one, own, met, passed, table, span)
    rel_sum = scatter_call([(ids_one, 1, dp_one)], rel_rows, [bf16], rel_part)
    rel_mine = relation_mine(rel_sum, axes)
    dl_one, rel_sum = lax.optimization_barrier((dl_one, rel_sum))
    left_one = scatter_call([(ids_one, 0, dl_one)], rows, [bf16])
    guest_left = send(left_one, neighbour, guest)
    d_right_one = scatter_call([(ids_one, 2, dt_one), (ids_one, 3, dc_one)], rows, [bf16], guest_left)
    back = send(d_right_one, parting)
    d_right_one, dt_two = lax.optimization_barrier((d_right_one, dt_two))
    d_right_two = scatter_call([(ids_two, 2, dt_two), (ids_two, 3, dc_two)], rows, [bf16])
    back_outer = send(d_right_two, lambda g, d: (g - 1, d))
    d_right_two, dl_two = lax.optimization_barrier((d_right_two, dl_two))
    left_two = scatter_call([(ids_two, 0, dl_two)], rows, [f32])
    entity_new, entity_acc_new = update_call(home, entity, entity_acc, left_two, back_outer, left_one, back)
    rel_total = relation_spread(rel_mine, axes)[:n_rel]
    rel_acc_new = rel_acc + jnp.mean(rel_total * rel_total, axis=1)
    relation_new = relation - learn_rate * rel_total / jnp.sqrt(rel_acc_new)[:, None]
    return (entity_new, entity_acc_new, relation_new, rel_acc_new)


def solution(mesh):
    return jax.shard_map(
        body,
        mesh=mesh,
        in_specs=(
            P(("grp", "dom"), None),
            P(("grp", "dom")),
            P(),
            P(),
            P(("grp", "dom"), None, None),
            P(("grp", "dom"), None, None),
            P(("grp", "dom"), None, None),
            P(("grp", "dom"), None, None, None),
        ),
        out_specs=(P(("grp", "dom"), None), P(("grp", "dom")), P(), P()),
        check_vma=False,
    )
```

```python
import jax
import jax.numpy as jnp
from jax import lax
from jax.experimental import pallas as pl
from jax.experimental.pallas import tpu as pltpu
from jax.sharding import PartitionSpec as P

learn_rate = 0.3
bf16 = jnp.bfloat16
f32 = jnp.float32
VMEM_LIMIT = 52 << 20


def dot_nn(a, b):
    return jnp.dot(a, b, preferred_element_type=f32)


def dot_nt(a, b):
    return lax.dot_general(a, b, (((1,), (1,)), ((), ())), preferred_element_type=f32)


def one_hot(ids, rows, first=0):
    shape = (rows, ids.shape[1])
    match = (ids - first).astype(jnp.int16) == lax.broadcasted_iota(jnp.int16, shape, 0)
    return jnp.where(match, jnp.ones((), bf16), jnp.zeros((), bf16))


def whole(shape):
    return pl.BlockSpec(shape, lambda s: (0,) * len(shape))


def across(height, width):
    return pl.BlockSpec((height, width), lambda s: (0, s))


def params():
    return pltpu.CompilerParams(dimension_semantics=("arbitrary",), vmem_limit_bytes=VMEM_LIMIT)


def halves(a):
    middle = a.shape[0] // 2
    return a[:middle], a[middle:]


def make_query(source, rel_ids, left, rel_table):
    features, rows = left.shape
    heads = dot_nn(left, one_hot(source, rows))
    both = dot_nn(rel_table, one_hot(rel_ids, rel_table.shape[1]))
    rel = both[:features] + both[features:]
    h_re, h_im = halves(heads)
    r_re, r_im = halves(rel)
    query = jnp.concatenate([h_re * r_re - h_im * r_im, h_re * r_im + h_im * r_re], 0)
    return heads, rel, query.astype(bf16)


def make_gradients(targets, negatives, heads, rel, query, right, heads_out, tails_out, cands_out, rels_out):
    rows = right.shape[1]
    tails = dot_nn(right, one_hot(targets, rows))
    cands = dot_nn(right, one_hot(negatives, rows)).astype(bf16)
    query32 = query.astype(f32)
    positive = jnp.sum(query32 * tails, axis=0, keepdims=True)
    scores = dot_nn(cands.T, query)
    peak = jnp.maximum(jnp.max(scores, axis=0, keepdims=True), positive)
    expd = jnp.exp(scores - peak)
    own = jnp.exp(positive - peak)
    inverse = 1.0 / (own + jnp.sum(expd, axis=0, keepdims=True))
    shares = (expd * inverse).astype(bf16)
    coefficient = own * inverse - 1.0
    tails_out[...] = (coefficient * query32).astype(bf16)
    cands_out[...] = dot_nt(query, shares).astype(bf16)
    grad = coefficient * tails + dot_nn(cands, shares)
    g_re, g_im = halves(grad)
    r_re, r_im = halves(rel)
    h_re, h_im = halves(heads)
    heads_out[...] = jnp.concatenate(
        [g_re * r_re + g_im * r_im, g_im * r_re - g_re * r_im], 0
    ).astype(bf16)
    rels_out[...] = jnp.concatenate(
        [g_re * h_re + g_im * h_im, g_im * h_re - g_re * h_im], 0
    ).astype(bf16)


def lines_kernel(source_ref, rel_ref, target_ref, negatives_ref, *outs):
    _, spans, _, span = negatives_ref.shape
    for bucket, out_ref in enumerate(outs):
        for line, ref in enumerate((source_ref, rel_ref, target_ref)):
            out_ref[line : line + 1] = ref[0, bucket : bucket + 1]
        for s in range(spans):
            out_ref[3:4, s * span : (s + 1) * span] = negatives_ref[0, s, bucket : bucket + 1]


def lines_call(*arrays):
    edges = arrays[0].shape[2]
    return pl.pallas_call(
        lines_kernel,
        in_specs=[pl.BlockSpec(memory_space=pltpu.VMEM)] * 4,
        out_specs=[pl.BlockSpec(memory_space=pltpu.VMEM)] * 2,
        out_shape=[jax.ShapeDtypeStruct((4, edges), jnp.int32)] * 2,
        cost_estimate=cost(1, 1, 1, 1),
        name="lines",
    )(*arrays)


def query_kernel(ids_ref, own_ref, relation_ref, heads_ref, rel_ref, query_ref, table_ref, left, padded):
    @pl.when(pl.program_id(0) == 0)
    def _():
        n_rel, features = relation_ref.shape
        left[...] = own_ref[...].T
        padded[:n_rel] = relation_ref[...]
        padded[n_rel:] = jnp.zeros((padded.shape[0] - n_rel, features), f32)
        across_rel = padded[...].T
        high = across_rel.astype(bf16)
        table_ref[:features] = high
        table_ref[features:] = (across_rel - high.astype(f32)).astype(bf16)

    ids = ids_ref[...]
    heads, rel, query = make_query(ids[0:1], ids[1:2], left[...], table_ref[...])
    heads_ref[...] = heads.astype(bf16)
    rel_ref[...] = rel
    query_ref[...] = query


def gradient_kernel(ids_ref, heads_ref, rel_ref, query_ref, partner_ref, *rest):
    *outs, right = rest

    @pl.when(pl.program_id(0) == 0)
    def _():
        right[...] = partner_ref[...].T

    ids = ids_ref[...]
    heads = heads_ref[...].astype(f32)
    make_gradients(ids[2:3], ids[3:4], heads, rel_ref[...], query_ref[...], right[...], *outs)


def paired_kernel(home_ref, ids_ref, own_ref, met_ref, passed_ref, table_ref, *rest):
    *outs, left, right = rest

    @pl.when(pl.program_id(0) == 0)
    def _():
        right[...] = met_ref[...].T

        @pl.when(home_ref[0] == 1)
        def _():
            left[...] = own_ref[...].T

        @pl.when(home_ref[0] == 0)
        def _():
            left[...] = passed_ref[...].T

    ids = ids_ref[...]
    heads, rel, query = make_query(ids[0:1], ids[1:2], left[...], table_ref[...])
    make_gradients(ids[2:3], ids[3:4], heads, rel, query, right[...], *outs)


def gradient_shapes(features, edges):
    return [jax.ShapeDtypeStruct((features, edges), bf16)] * 4


def gradient_specs(features, span):
    return [across(features, span)] * 4


def cost(units, span, features, rows):
    return pl.CostEstimate(flops=1 << 40, bytes_accessed=1 << 32, transcendentals=0)


def query_call(ids, own, relation, rel_rows, span):
    edges = ids.shape[1]
    rows, features = own.shape
    return pl.pallas_call(
        query_kernel,
        grid=(edges // span,),
        in_specs=[across(4, span), whole(own.shape), whole(relation.shape)],
        out_specs=[across(features, span)] * 3 + [whole((2 * features, rel_rows))],
        out_shape=[
            jax.ShapeDtypeStruct((features, edges), bf16),
            jax.ShapeDtypeStruct((features, edges), f32),
            jax.ShapeDtypeStruct((features, edges), bf16),
            jax.ShapeDtypeStruct((2 * features, rel_rows), bf16),
        ],
        scratch_shapes=[pltpu.VMEM((features, rows), bf16), pltpu.VMEM((rel_rows, features), f32)],
        compiler_params=params(),
        cost_estimate=cost(2, edges, features, rows),
        name="queries",
    )(ids, own, relation)


def gradient_call(ids, heads, rel, query, partner, span):
    features, edges = heads.shape
    rows = partner.shape[0]
    return pl.pallas_call(
        gradient_kernel,
        grid=(edges // span,),
        in_specs=[across(4, span)] + [across(features, span)] * 3 + [whole(partner.shape)],
        out_specs=gradient_specs(features, span),
        out_shape=gradient_shapes(features, edges),
        scratch_shapes=[pltpu.VMEM((features, rows), bf16)],
        compiler_params=params(),
        cost_estimate=cost(3, edges, features, rows),
        name="gradients",
    )(ids, heads, rel, query, partner)


def paired_call(home, ids, own, met, passed, table, span):
    edges = ids.shape[1]
    rows, features = own.shape
    return pl.pallas_call(
        paired_kernel,
        grid=(edges // span,),
        in_specs=[pl.BlockSpec(memory_space=pltpu.SMEM), across(4, span)]
        + [whole(own.shape)] * 3
        + [whole(table.shape)],
        out_specs=gradient_specs(features, span),
        out_shape=gradient_shapes(features, edges),
        scratch_shapes=[pltpu.VMEM((features, rows), bf16)] * 2,
        compiler_params=params(),
        cost_estimate=cost(5, edges, features, rows),
        name="paired",
    )(home, ids, own, met, passed, table)


def scatter_kernel(chunk, lines, n_starts, *refs):
    first = pl.program_id(0) * chunk
    n_pairs = len(lines)
    ins = 2 * n_pairs + n_starts
    total = None
    for k, line in enumerate(lines):
        part = dot_nt(one_hot(refs[2 * k][line : line + 1, :], chunk, first), refs[2 * k + 1][...])
        total = part if total is None else total + part
    for start in refs[2 * n_pairs : ins]:
        total = total + start[...].astype(f32)
    for out_ref in refs[ins:]:
        out_ref[...] = total.astype(out_ref.dtype)


def scatter_call(pairs, rows, dtypes, starts=(), chunk=512):
    features = pairs[0][2].shape[0]
    chunk = min(chunk, rows)
    operands, specs = [], []
    for ids, _, vectors in pairs:
        operands += [ids, vectors]
        specs += [whole(ids.shape), whole(vectors.shape)]
    down = pl.BlockSpec((chunk, features), lambda s: (s, 0))
    for start in starts:
        operands.append(start)
        specs.append(down)

    def kernel(*refs):
        scatter_kernel(chunk, [line for _, line, _ in pairs], len(starts), *refs)

    outs = pl.pallas_call(
        kernel,
        grid=(rows // chunk,),
        in_specs=specs,
        out_specs=[down] * len(dtypes),
        out_shape=[jax.ShapeDtypeStruct((rows, features), dtype) for dtype in dtypes],
        compiler_params=params(),
        cost_estimate=cost(1, sum(v.shape[1] for _, _, v in pairs), features, rows),
        name="scatter",
    )(*operands)
    return outs[0] if len(outs) == 1 else outs


def adagrad_lines(grad, acc):
    rows = grad.shape[0]
    mean = jnp.mean(grad * grad, axis=1, keepdims=True)
    acc_new = acc + jnp.broadcast_to(mean, (rows, 128)).T[:1]
    scale = learn_rate / jnp.sqrt(acc_new)
    return acc_new, jnp.broadcast_to(scale, (128, rows)).T[:, :1]


def update_kernel(home_ref, entity_ref, acc_ref, local_ref, outer_ref, inner_ref, back_ref, new_ref, acc_new_ref):
    grad = local_ref[...] + outer_ref[...].astype(f32) + back_ref[...].astype(f32)
    grad = grad + jnp.where(home_ref[0] == 1, inner_ref[...].astype(f32), 0.0)
    acc_new, scale = adagrad_lines(grad, acc_ref[...])
    acc_new_ref[...] = acc_new
    new_ref[...] = (entity_ref[...].astype(f32) - scale * grad).astype(bf16)


def update_call(home, entity, acc, local, outer, inner, back, chunk=512):
    rows, features = entity.shape
    down = pl.BlockSpec((chunk, features), lambda s: (s, 0))
    line = pl.BlockSpec((1, chunk), lambda s: (0, s))
    new, acc_new = pl.pallas_call(
        update_kernel,
        grid=(rows // chunk,),
        in_specs=[pl.BlockSpec(memory_space=pltpu.SMEM), down, line, down, down, down, down],
        out_specs=[down, line],
        out_shape=[jax.ShapeDtypeStruct((rows, features), bf16), jax.ShapeDtypeStruct((1, rows), f32)],
        compiler_params=params(),
        cost_estimate=cost(1, rows, features, rows),
        name="update",
    )(home, entity, acc.reshape(1, rows), local, outer, inner, back)
    return new, acc_new.reshape(rows)


def relation_kernel(relation_ref, acc_ref, total_ref, new_ref, acc_new_ref):
    n_rel = relation_ref.shape[0]
    total = total_ref[...].astype(f32)
    acc_new, scale = adagrad_lines(total, acc_ref[...])
    acc_new_ref[...] = acc_new[:, :n_rel]
    new_ref[...] = relation_ref[...] - scale[:n_rel] * total[:n_rel]


def relation_call(relation, acc, total):
    n_rel = relation.shape[0]
    line = jnp.pad(acc.reshape(1, n_rel), ((0, 0), (0, total.shape[0] - n_rel)), constant_values=1.0)
    new, acc_new = pl.pallas_call(
        relation_kernel,
        in_specs=[pl.BlockSpec(memory_space=pltpu.VMEM)] * 3,
        out_specs=[pl.BlockSpec(memory_space=pltpu.VMEM)] * 2,
        out_shape=[jax.ShapeDtypeStruct(relation.shape, f32), jax.ShapeDtypeStruct((1, n_rel), f32)],
        compiler_params=pltpu.CompilerParams(vmem_limit_bytes=VMEM_LIMIT),
        cost_estimate=cost(1, 1, 1, 1),
        name="relation",
    )(relation, line, total)
    return new, acc_new.reshape(n_rel)


def shares_kernel(pieces_ref, out_ref):
    share = jnp.sum(pieces_ref[...].astype(f32), axis=0).astype(bf16)
    for k in range(out_ref.shape[0]):
        out_ref[k] = share


def shares_call(pieces, copies):
    return pl.pallas_call(
        shares_kernel,
        in_specs=[pl.BlockSpec(memory_space=pltpu.VMEM)],
        out_specs=pl.BlockSpec(memory_space=pltpu.VMEM),
        out_shape=jax.ShapeDtypeStruct((copies,) + pieces.shape[1:], bf16),
        cost_estimate=cost(1, 1, 1, 1),
        name="shares",
    )(pieces)


def body(entity, entity_acc, relation, rel_acc, edge_src, edge_rel, edge_dst, negatives):
    axes = ("grp", "dom")
    groups, doms = lax.axis_size("grp"), lax.axis_size("dom")
    half = doms // 2
    rows, features = entity.shape
    n_rel = relation.shape[0]
    spans, span = negatives.shape[2:]
    edges = spans * span
    step = max(128, 8 * groups * doms)
    rel_rows = -(-n_rel // step) * step

    places = [(g, d) for g in range(groups) for d in range(doms)]

    def is_home(g, d):
        return g % 2 == d // half

    def send(block, to, only=lambda g, d: True):
        route = []
        for g, d in places:
            if only(g, d):
                h, e = to(g, d)
                route.append((g * doms + d, h % groups * doms + e % doms))
        return lax.ppermute(block, axes, route)

    def guest(g, d):
        return not is_home(g, d)

    def meeting(g, d):
        return (g ^ 1, d) if is_home(g, d) else (g, d + half)

    def parting(g, d):
        return (g, d + half) if is_home(g, d) else (g ^ 1, d)

    def neighbour(g, d):
        return g ^ 1, d

    home = (lax.axis_index("grp") % 2 == lax.axis_index("dom") // half).astype(jnp.int32).reshape(1)

    ids_one, ids_two = lines_call(edge_src, edge_rel, edge_dst, negatives.transpose(0, 2, 1, 3))
    met = send(entity, meeting)
    outer = send(entity, lambda g, d: (g + 1, d))
    heads, rel, query, table = query_call(ids_two, entity, relation, rel_rows, span)
    dl_two, dt_two, dc_two, dp_two = gradient_call(ids_two, heads, rel, query, outer, span)
    met, ids_one, dt_two = lax.optimization_barrier((met, ids_one, dt_two))
    passed = send(met, neighbour, is_home)
    sent_ids = send(ids_one, lambda g, d: (g ^ 1, d + half), guest)
    rel_part = scatter_call([(ids_two, 1, dp_two)], rel_rows, [f32])
    passed, sent_ids, rel_part = lax.optimization_barrier((passed, sent_ids, rel_part))
    ids_one = jnp.where(home == 1, ids_one, sent_ids)
    dl_one, dt_one, dc_one, dp_one = paired_call(home, ids_one, entity, met, passed, table, span)

    left_one = scatter_call([(ids_one, 0, dl_one)], rows, [bf16])
    guest_left = send(left_one, neighbour, guest)
    d_right_one = scatter_call([(ids_one, 2, dt_one), (ids_one, 3, dc_one)], rows, [bf16], [guest_left])
    back = send(d_right_one, parting)
    d_right_one, dp_one, dt_two, dl_two = lax.optimization_barrier((d_right_one, dp_one, dt_two, dl_two))

    planes = [[g * doms + q + x for g in range(groups) for x in range(2)] for q in range(0, doms, 2)]
    stacks = [[g * doms + q + x for q in range(0, doms, 2)] for g in range(groups) for x in range(2)]

    def exchange(pieces, sets):
        return lax.all_to_all(pieces, axes, 0, 0, axis_index_groups=sets, tiled=True)

    rel_sum = scatter_call([(ids_one, 1, dp_one)], rel_rows, [bf16], [rel_part])
    shares = exchange(rel_sum.reshape(2 * groups, -1, features), planes)
    rel_sum, dt_two = lax.optimization_barrier((rel_sum, dt_two))
    d_right_two = scatter_call([(ids_two, 2, dt_two), (ids_two, 3, dc_two)], rows, [bf16])
    back_outer = send(d_right_two, lambda g, d: (g - 1, d))
    shares, d_right_two = lax.optimization_barrier((shares, d_right_two))
    shares = exchange(shares_call(shares, len(stacks[0])), stacks)
    d_right_two, dl_two = lax.optimization_barrier((d_right_two, dl_two))
    local = scatter_call([(ids_two, 0, dl_two)], rows, [f32])
    shares, local = lax.optimization_barrier((shares, local))
    total = exchange(shares_call(shares, len(planes[0])), planes).reshape(rel_rows, features)
    entity_new, entity_acc_new = update_call(home, entity, entity_acc, local, back_outer, left_one, back)
    relation_new, rel_acc_new = relation_call(relation, rel_acc, total)
    return (entity_new, entity_acc_new, relation_new, rel_acc_new)


def solution(mesh):
    return jax.shard_map(
        body,
        mesh=mesh,
        in_specs=(
            P(("grp", "dom"), None),
            P(("grp", "dom")),
            P(),
            P(),
            P(("grp", "dom"), None, None),
            P(("grp", "dom"), None, None),
            P(("grp", "dom"), None, None),
            P(("grp", "dom"), None, None, None),
        ),
        out_specs=(P(("grp", "dom"), None), P(("grp", "dom")), P(), P()),
        check_vma=False,
    )
```

```python
import functools

import jax
import jax.numpy as jnp
from jax import lax
from jax.experimental import pallas as pl
from jax.experimental.pallas import tpu as pltpu
from jax.sharding import PartitionSpec as P

learn_rate = 0.3
bf16 = jnp.bfloat16
f32 = jnp.float32
VMEM_LIMIT = 52 << 20


def dot_nn(a, b):
    return jnp.dot(a, b, preferred_element_type=f32)


def dot_nt(a, b):
    return lax.dot_general(a, b, (((1,), (1,)), ((), ())), preferred_element_type=f32)


def one_hot(ids, rows, first=0):
    shape = (rows, ids.shape[1])
    match = (ids - first).astype(jnp.int16) == lax.broadcasted_iota(jnp.int16, shape, 0)
    return jnp.where(match, jnp.ones((), bf16), jnp.zeros((), bf16))


def whole(shape):
    return pl.BlockSpec(shape, lambda s: (0,) * len(shape))


def across(height, width):
    return pl.BlockSpec((height, width), lambda s: (0, s))


def params():
    return pltpu.CompilerParams(dimension_semantics=("arbitrary",), vmem_limit_bytes=VMEM_LIMIT)


def halves(a):
    middle = a.shape[0] // 2
    return a[:middle], a[middle:]


def make_query(source, rel_ids, left, rel_table):
    features, rows = left.shape
    heads = dot_nn(left, one_hot(source, rows))
    both = dot_nn(rel_table, one_hot(rel_ids, rel_table.shape[1]))
    rel = both[:features] + both[features:]
    h_re, h_im = halves(heads)
    r_re, r_im = halves(rel)
    query = jnp.concatenate([h_re * r_re - h_im * r_im, h_re * r_im + h_im * r_re], 0)
    return heads, rel, query.astype(bf16)


def make_gradients(span, targets, negatives, heads, rel, query, right, outs):
    width = query.shape[1]
    rows = right.shape[1]
    picked = dot_nn(right, one_hot(jnp.concatenate([targets, negatives], axis=1), rows))
    for first in range(0, width, span):
        part = slice(first, first + span)
        tails = picked[:, part]
        cands = picked[:, width + first : width + first + span].astype(bf16)
        span_gradients(tails, cands, heads[:, part], rel[:, part], query[:, part], [o.at[:, part] for o in outs])


def span_gradients(tails, cands, heads, rel, query, outs):
    heads_out, tails_out, cands_out, rels_out = outs
    query32 = query.astype(f32)
    positive = jnp.sum(query32 * tails, axis=0, keepdims=True)
    scores = dot_nn(cands.T, query)
    peak = jnp.maximum(jnp.max(scores, axis=0, keepdims=True), positive)
    expd = jnp.exp(scores - peak)
    own = jnp.exp(positive - peak)
    inverse = 1.0 / (own + jnp.sum(expd, axis=0, keepdims=True))
    shares = (expd * inverse).astype(bf16)
    coefficient = own * inverse - 1.0
    tails_out[...] = (coefficient * query32).astype(bf16)
    cands_out[...] = dot_nt(query, shares).astype(bf16)
    grad = coefficient * tails + dot_nn(cands, shares)
    g_re, g_im = halves(grad)
    r_re, r_im = halves(rel)
    h_re, h_im = halves(heads)
    heads_out[...] = jnp.concatenate(
        [g_re * r_re + g_im * r_im, g_im * r_re - g_re * r_im], 0
    ).astype(bf16)
    rels_out[...] = jnp.concatenate(
        [g_re * h_re + g_im * h_im, g_im * h_re - g_re * h_im], 0
    ).astype(bf16)


def lines_kernel(source_ref, rel_ref, target_ref, negatives_ref, *outs):
    _, spans, _, span = negatives_ref.shape
    for bucket, out_ref in enumerate(outs):
        for line, ref in enumerate((source_ref, rel_ref, target_ref)):
            out_ref[line : line + 1] = ref[0, bucket : bucket + 1]
        for s in range(spans):
            out_ref[3:4, s * span : (s + 1) * span] = negatives_ref[0, s, bucket : bucket + 1]


def lines_call(*arrays):
    edges = arrays[0].shape[2]
    return pl.pallas_call(
        lines_kernel,
        in_specs=[pl.BlockSpec(memory_space=pltpu.VMEM)] * 4,
        out_specs=[pl.BlockSpec(memory_space=pltpu.VMEM)] * 2,
        out_shape=[jax.ShapeDtypeStruct((4, edges), jnp.int32)] * 2,
        cost_estimate=cost(1, 1, 1, 1),
        name="lines",
    )(*arrays)


def query_kernel(ids_ref, own_ref, relation_ref, heads_ref, rel_ref, query_ref, table_ref, left, padded):
    @pl.when(pl.program_id(0) == 0)
    def _():
        n_rel, features = relation_ref.shape
        left[...] = own_ref[...].T
        padded[:n_rel] = relation_ref[...]
        padded[n_rel:] = jnp.zeros((padded.shape[0] - n_rel, features), f32)
        across_rel = padded[...].T
        high = across_rel.astype(bf16)
        table_ref[:features] = high
        table_ref[features:] = (across_rel - high.astype(f32)).astype(bf16)

    ids = ids_ref[...]
    heads, rel, query = make_query(ids[0:1], ids[1:2], left[...], table_ref[...])
    heads_ref[...] = heads.astype(bf16)
    rel_ref[...] = rel
    query_ref[...] = query


def gradient_kernel(span, ids_ref, heads_ref, rel_ref, query_ref, partner_ref, *rest):
    *outs, right = rest

    @pl.when(pl.program_id(0) == 0)
    def _():
        right[...] = partner_ref[...].T

    ids = ids_ref[...]
    heads = heads_ref[...].astype(f32)
    make_gradients(span, ids[2:3], ids[3:4], heads, rel_ref[...], query_ref[...], right[...], outs)


def paired_kernel(span, home_ref, ids_ref, sent_ref, own_ref, met_ref, passed_ref, table_ref, *rest):
    *outs, ids_out, left, right = rest

    @pl.when(pl.program_id(0) == 0)
    def _():
        right[...] = met_ref[...].T

        @pl.when(home_ref[0] == 1)
        def _():
            left[...] = own_ref[...].T

        @pl.when(home_ref[0] == 0)
        def _():
            left[...] = passed_ref[...].T

    ids = jnp.where(home_ref[0] == 1, ids_ref[...], sent_ref[...])
    ids_out[...] = ids
    heads, rel, query = make_query(ids[0:1], ids[1:2], left[...], table_ref[...])
    make_gradients(span, ids[2:3], ids[3:4], heads, rel, query, right[...], outs)


def gradient_shapes(features, edges):
    return [jax.ShapeDtypeStruct((features, edges), bf16)] * 4


def gradient_specs(features, span):
    return [across(features, span)] * 4


def cost(units, span, features, rows):
    return pl.CostEstimate(flops=1 << 40, bytes_accessed=1 << 32, transcendentals=0)


def query_call(ids, own, relation, rel_rows, width):
    edges = ids.shape[1]
    rows, features = own.shape
    return pl.pallas_call(
        query_kernel,
        grid=(edges // width,),
        in_specs=[across(4, width), whole(own.shape), whole(relation.shape)],
        out_specs=[across(features, width)] * 3 + [whole((2 * features, rel_rows))],
        out_shape=[
            jax.ShapeDtypeStruct((features, edges), bf16),
            jax.ShapeDtypeStruct((features, edges), f32),
            jax.ShapeDtypeStruct((features, edges), bf16),
            jax.ShapeDtypeStruct((2 * features, rel_rows), bf16),
        ],
        scratch_shapes=[pltpu.VMEM((features, rows), bf16), pltpu.VMEM((rel_rows, features), f32)],
        compiler_params=params(),
        cost_estimate=cost(2, edges, features, rows),
        name="queries",
    )(ids, own, relation)


def gradient_call(ids, heads, rel, query, partner, span, width):
    features, edges = heads.shape
    rows = partner.shape[0]
    return pl.pallas_call(
        functools.partial(gradient_kernel, span),
        grid=(edges // width,),
        in_specs=[across(4, width)] + [across(features, width)] * 3 + [whole(partner.shape)],
        out_specs=gradient_specs(features, width),
        out_shape=gradient_shapes(features, edges),
        scratch_shapes=[pltpu.VMEM((features, rows), bf16)],
        compiler_params=params(),
        cost_estimate=cost(3, edges, features, rows),
        name="gradients",
    )(ids, heads, rel, query, partner)


def paired_call(home, ids, sent_ids, own, met, passed, table, span, width):
    edges = ids.shape[1]
    rows, features = own.shape
    return pl.pallas_call(
        functools.partial(paired_kernel, span),
        grid=(edges // width,),
        in_specs=[pl.BlockSpec(memory_space=pltpu.SMEM), across(4, width), across(4, width)]
        + [whole(own.shape)] * 3
        + [whole(table.shape)],
        out_specs=gradient_specs(features, width) + [across(4, width)],
        out_shape=gradient_shapes(features, edges) + [jax.ShapeDtypeStruct(ids.shape, jnp.int32)],
        scratch_shapes=[pltpu.VMEM((features, rows), bf16)] * 2,
        compiler_params=params(),
        cost_estimate=cost(5, edges, features, rows),
        name="paired",
    )(home, ids, sent_ids, own, met, passed, table)


def scatter_kernel(chunk, lines, n_starts, *refs):
    first = pl.program_id(0) * chunk
    n_pairs = len(lines)
    ins = 2 * n_pairs + n_starts
    total = None
    for k, line in enumerate(lines):
        part = dot_nt(one_hot(refs[2 * k][line : line + 1, :], chunk, first), refs[2 * k + 1][...])
        total = part if total is None else total + part
    for start in refs[2 * n_pairs : ins]:
        total = total + start[...].astype(f32)
    for out_ref in refs[ins:]:
        out_ref[...] = total.astype(out_ref.dtype)


def scatter_call(pairs, rows, dtypes, starts=(), chunk=512):
    features = pairs[0][2].shape[0]
    chunk = min(chunk, rows)
    operands, specs = [], []
    for ids, _, vectors in pairs:
        operands += [ids, vectors]
        specs += [whole(ids.shape), whole(vectors.shape)]
    down = pl.BlockSpec((chunk, features), lambda s: (s, 0))
    for start in starts:
        operands.append(start)
        specs.append(down)

    def kernel(*refs):
        scatter_kernel(chunk, [line for _, line, _ in pairs], len(starts), *refs)

    outs = pl.pallas_call(
        kernel,
        grid=(rows // chunk,),
        in_specs=specs,
        out_specs=[down] * len(dtypes),
        out_shape=[jax.ShapeDtypeStruct((rows, features), dtype) for dtype in dtypes],
        compiler_params=params(),
        cost_estimate=cost(1, sum(v.shape[1] for _, _, v in pairs), features, rows),
        name="scatter",
    )(*operands)
    return outs[0] if len(outs) == 1 else outs


def adagrad(grad, acc):
    rows, features = grad.shape
    mean = jnp.mean(grad * grad, axis=1, keepdims=True)
    acc_new = jnp.broadcast_to(acc, (128, rows)).T + mean
    scale = learn_rate / jnp.sqrt(acc_new)
    steps = [grad[:, k : k + 128] * scale for k in range(0, features, 128)]
    return acc_new.T[:1], jnp.concatenate(steps, axis=1)


def update_kernel(home_ref, entity_ref, acc_ref, local_ref, outer_ref, inner_ref, back_ref, new_ref, acc_new_ref):
    grad = local_ref[...] + outer_ref[...].astype(f32) + back_ref[...].astype(f32)
    grad = grad + jnp.where(home_ref[0] == 1, inner_ref[...].astype(f32), 0.0)
    acc_new, step = adagrad(grad, acc_ref[...])
    acc_new_ref[...] = acc_new
    new_ref[...] = (entity_ref[...].astype(f32) - step).astype(bf16)


def update_call(home, entity, acc, local, outer, inner, back, chunk=512):
    rows, features = entity.shape
    down = pl.BlockSpec((chunk, features), lambda s: (s, 0))
    line = pl.BlockSpec((1, chunk), lambda s: (0, s))
    new, acc_new = pl.pallas_call(
        update_kernel,
        grid=(rows // chunk,),
        in_specs=[pl.BlockSpec(memory_space=pltpu.SMEM), down, line, down, down, down, down],
        out_specs=[down, line],
        out_shape=[jax.ShapeDtypeStruct((rows, features), bf16), jax.ShapeDtypeStruct((1, rows), f32)],
        compiler_params=params(),
        cost_estimate=cost(1, rows, features, rows),
        name="update",
    )(home, entity, acc.reshape(1, rows), local, outer, inner, back)
    return new, acc_new.reshape(rows)


def relation_kernel(relation_ref, acc_ref, total_ref, new_ref, acc_new_ref):
    n_rel = relation_ref.shape[0]
    total = total_ref[...].astype(f32)
    acc_new, step = adagrad(total, acc_ref[...])
    acc_new_ref[...] = acc_new[:, :n_rel]
    new_ref[...] = relation_ref[...] - step[:n_rel]


def relation_call(relation, acc, total):
    n_rel = relation.shape[0]
    line = jnp.pad(acc.reshape(1, n_rel), ((0, 0), (0, total.shape[0] - n_rel)), constant_values=1.0)
    new, acc_new = pl.pallas_call(
        relation_kernel,
        in_specs=[pl.BlockSpec(memory_space=pltpu.VMEM)] * 3,
        out_specs=[pl.BlockSpec(memory_space=pltpu.VMEM)] * 2,
        out_shape=[jax.ShapeDtypeStruct(relation.shape, f32), jax.ShapeDtypeStruct((1, n_rel), f32)],
        compiler_params=pltpu.CompilerParams(vmem_limit_bytes=VMEM_LIMIT),
        cost_estimate=cost(1, 1, 1, 1),
        name="relation",
    )(relation, line, total)
    return new, acc_new.reshape(n_rel)


def shares_kernel(pieces_ref, out_ref):
    share = jnp.sum(pieces_ref[...].astype(f32), axis=0).astype(bf16)
    for k in range(out_ref.shape[0]):
        out_ref[k] = share


def shares_call(pieces, copies):
    return pl.pallas_call(
        shares_kernel,
        in_specs=[pl.BlockSpec(memory_space=pltpu.VMEM)],
        out_specs=pl.BlockSpec(memory_space=pltpu.VMEM),
        out_shape=jax.ShapeDtypeStruct((copies,) + pieces.shape[1:], bf16),
        cost_estimate=cost(1, 1, 1, 1),
        name="shares",
    )(pieces)


def body(entity, entity_acc, relation, rel_acc, edge_src, edge_rel, edge_dst, negatives):
    axes = ("grp", "dom")
    groups, doms = lax.axis_size("grp"), lax.axis_size("dom")
    half = doms // 2
    rows, features = entity.shape
    n_rel = relation.shape[0]
    spans, span = negatives.shape[2:]
    edges = spans * span
    width = span * (2 - spans % 2)
    step = max(128, 8 * groups * doms)
    rel_rows = -(-n_rel // step) * step

    places = [(g, d) for g in range(groups) for d in range(doms)]

    def is_home(g, d):
        return g % 2 == d // half

    def send(block, to, only=lambda g, d: True):
        route = []
        for g, d in places:
            if only(g, d):
                h, e = to(g, d)
                route.append((g * doms + d, h % groups * doms + e % doms))
        return lax.ppermute(block, axes, route)

    def guest(g, d):
        return not is_home(g, d)

    def meeting(g, d):
        return (g ^ 1, d) if is_home(g, d) else (g, d + half)

    def parting(g, d):
        return (g, d + half) if is_home(g, d) else (g ^ 1, d)

    def neighbour(g, d):
        return g ^ 1, d

    home = (lax.axis_index("grp") % 2 == lax.axis_index("dom") // half).astype(jnp.int32).reshape(1)

    ids_one, ids_two = lines_call(edge_src, edge_rel, edge_dst, negatives.transpose(0, 2, 1, 3))
    met = send(entity, meeting)
    outer = send(entity, lambda g, d: (g + 1, d))
    heads, rel, query, table = query_call(ids_two, entity, relation, rel_rows, width)
    dl_two, dt_two, dc_two, dp_two = gradient_call(ids_two, heads, rel, query, outer, span, width)
    met, ids_one, dt_two = lax.optimization_barrier((met, ids_one, dt_two))
    passed = send(met, neighbour, is_home)
    sent_ids = send(ids_one, lambda g, d: (g ^ 1, d + half), guest)
    rel_part = scatter_call([(ids_two, 1, dp_two)], rel_rows, [f32])
    passed, sent_ids, rel_part = lax.optimization_barrier((passed, sent_ids, rel_part))
    dl_one, dt_one, dc_one, dp_one, ids_one = paired_call(
        home, ids_one, sent_ids, entity, met, passed, table, span, width
    )

    left_one = scatter_call([(ids_one, 0, dl_one)], rows, [bf16])
    guest_left = send(left_one, neighbour, guest)
    d_right_one = scatter_call([(ids_one, 2, dt_one), (ids_one, 3, dc_one)], rows, [bf16], [guest_left])
    back = send(d_right_one, parting)
    d_right_one, dp_one, dt_two, dl_two = lax.optimization_barrier((d_right_one, dp_one, dt_two, dl_two))

    planes = [[g * doms + q + x for g in range(groups) for x in range(2)] for q in range(0, doms, 2)]
    stacks = [[g * doms + q + x for q in range(0, doms, 2)] for g in range(groups) for x in range(2)]

    def exchange(pieces, sets):
        return lax.all_to_all(pieces, axes, 0, 0, axis_index_groups=sets, tiled=True)

    rel_sum = scatter_call([(ids_one, 1, dp_one)], rel_rows, [bf16], [rel_part])
    shares = exchange(rel_sum.reshape(2 * groups, -1, features), planes)
    rel_sum, dt_two = lax.optimization_barrier((rel_sum, dt_two))
    d_right_two = scatter_call([(ids_two, 2, dt_two), (ids_two, 3, dc_two)], rows, [bf16])
    back_outer = send(d_right_two, lambda g, d: (g - 1, d))
    shares, d_right_two = lax.optimization_barrier((shares, d_right_two))
    shares = exchange(shares_call(shares, len(stacks[0])), stacks)
    d_right_two, dl_two = lax.optimization_barrier((d_right_two, dl_two))
    local = scatter_call([(ids_two, 0, dl_two)], rows, [f32])
    shares, local = lax.optimization_barrier((shares, local))
    total = exchange(shares_call(shares, len(planes[0])), planes).reshape(rel_rows, features)
    entity_new, entity_acc_new = update_call(home, entity, entity_acc, local, back_outer, left_one, back)
    relation_new, rel_acc_new = relation_call(relation, rel_acc, total)
    return (entity_new, entity_acc_new, relation_new, rel_acc_new)


def solution(mesh):
    return jax.shard_map(
        body,
        mesh=mesh,
        in_specs=(
            P(("grp", "dom"), None),
            P(("grp", "dom")),
            P(),
            P(),
            P(("grp", "dom"), None, None),
            P(("grp", "dom"), None, None),
            P(("grp", "dom"), None, None),
            P(("grp", "dom"), None, None, None),
        ),
        out_specs=(P(("grp", "dom"), None), P(("grp", "dom")), P(), P()),
        check_vma=False,
    )
```

```python
import functools

import jax
import jax.numpy as jnp
from jax import lax
from jax.experimental import pallas as pl
from jax.experimental.pallas import tpu as pltpu
from jax.sharding import PartitionSpec as P

learn_rate = 0.3
bf16 = jnp.bfloat16
f32 = jnp.float32
VMEM_LIMIT = 52 << 20


def dot_nn(a, b):
    return jnp.dot(a, b, preferred_element_type=f32)


def dot_nt(a, b):
    return lax.dot_general(a, b, (((1,), (1,)), ((), ())), preferred_element_type=f32)


def one_hot(ids, rows, first=0):
    shape = (rows, ids.shape[1])
    match = (ids - first).astype(jnp.int16) == lax.broadcasted_iota(jnp.int16, shape, 0)
    return jnp.where(match, jnp.ones((), bf16), jnp.zeros((), bf16))


def whole(shape):
    return pl.BlockSpec(shape, lambda s: (0,) * len(shape))


def across(height, width):
    return pl.BlockSpec((height, width), lambda s: (0, s))


def params():
    return pltpu.CompilerParams(dimension_semantics=("arbitrary",), vmem_limit_bytes=VMEM_LIMIT)


def halves(a):
    middle = a.shape[0] // 2
    return a[:middle], a[middle:]


def make_query(source, rel_ids, left, rel_table):
    features, rows = left.shape
    heads = dot_nn(left, one_hot(source, rows))
    both = dot_nn(rel_table, one_hot(rel_ids, rel_table.shape[1]))
    rel = both[:features] + both[features:]
    h_re, h_im = halves(heads)
    r_re, r_im = halves(rel)
    query = jnp.concatenate([h_re * r_re - h_im * r_im, h_re * r_im + h_im * r_re], 0)
    return heads, rel, query.astype(bf16)


def make_gradients(span, targets, negatives, heads, rel, query, right, outs):
    width = query.shape[1]
    rows = right.shape[1]
    picked = dot_nn(right, one_hot(jnp.concatenate([targets, negatives], axis=1), rows))
    for first in range(0, width, span):
        part = slice(first, first + span)
        tails = picked[:, part]
        cands = picked[:, width + first : width + first + span].astype(bf16)
        span_gradients(tails, cands, heads[:, part], rel[:, part], query[:, part], [o.at[:, part] for o in outs])


def span_gradients(tails, cands, heads, rel, query, outs):
    heads_out, tails_out, cands_out, rels_out = outs
    query32 = query.astype(f32)
    positive = jnp.sum(query32 * tails, axis=0, keepdims=True)
    scores = dot_nn(cands.T, query)
    peak = jnp.maximum(jnp.max(scores, axis=0, keepdims=True), positive)
    expd = jnp.exp(scores - peak)
    own = jnp.exp(positive - peak)
    inverse = 1.0 / (own + jnp.sum(expd, axis=0, keepdims=True))
    shares = (expd * inverse).astype(bf16)
    coefficient = own * inverse - 1.0
    tails_out[...] = (coefficient * query32).astype(bf16)
    cands_out[...] = dot_nt(query, shares).astype(bf16)
    grad = coefficient * tails + dot_nn(cands, shares)
    g_re, g_im = halves(grad)
    r_re, r_im = halves(rel)
    h_re, h_im = halves(heads)
    heads_out[...] = jnp.concatenate(
        [g_re * r_re + g_im * r_im, g_im * r_re - g_re * r_im], 0
    ).astype(bf16)
    rels_out[...] = jnp.concatenate(
        [g_re * h_re + g_im * h_im, g_im * h_re - g_re * h_im], 0
    ).astype(bf16)


def lines_kernel(source_ref, rel_ref, target_ref, negatives_ref, *outs):
    _, spans, _, span = negatives_ref.shape
    for bucket, out_ref in enumerate(outs):
        for line, ref in enumerate((source_ref, rel_ref, target_ref)):
            out_ref[line : line + 1] = ref[0, bucket : bucket + 1]
        for s in range(spans):
            out_ref[3:4, s * span : (s + 1) * span] = negatives_ref[0, s, bucket : bucket + 1]


def lines_call(*arrays):
    edges = arrays[0].shape[2]
    return pl.pallas_call(
        lines_kernel,
        in_specs=[pl.BlockSpec(memory_space=pltpu.VMEM)] * 4,
        out_specs=[pl.BlockSpec(memory_space=pltpu.VMEM)] * 2,
        out_shape=[jax.ShapeDtypeStruct((4, edges), jnp.int32)] * 2,
        cost_estimate=cost(1, 1, 1, 1),
        name="lines",
    )(*arrays)


def query_kernel(ids_ref, own_ref, relation_ref, heads_ref, rel_ref, query_ref, table_ref, left, padded):
    @pl.when(pl.program_id(0) == 0)
    def _():
        n_rel, features = relation_ref.shape
        left[...] = own_ref[...].T
        padded[:n_rel] = relation_ref[...]
        padded[n_rel:] = jnp.zeros((padded.shape[0] - n_rel, features), f32)
        across_rel = padded[...].T
        high = across_rel.astype(bf16)
        table_ref[:features] = high
        table_ref[features:] = (across_rel - high.astype(f32)).astype(bf16)

    ids = ids_ref[...]
    heads, rel, query = make_query(ids[0:1], ids[1:2], left[...], table_ref[...])
    heads_ref[...] = heads.astype(bf16)
    rel_ref[...] = rel
    query_ref[...] = query


def gradient_kernel(span, ids_ref, heads_ref, rel_ref, query_ref, partner_ref, *rest):
    *outs, right = rest

    @pl.when(pl.program_id(0) == 0)
    def _():
        right[...] = partner_ref[...].T

    ids = ids_ref[...]
    heads = heads_ref[...].astype(f32)
    make_gradients(span, ids[2:3], ids[3:4], heads, rel_ref[...], query_ref[...], right[...], outs)


def paired_kernel(span, home_ref, ids_ref, sent_ref, own_ref, met_ref, passed_ref, table_ref, *rest):
    *outs, ids_out, left, right = rest

    @pl.when(pl.program_id(0) == 0)
    def _():
        right[...] = met_ref[...].T

        @pl.when(home_ref[0] == 1)
        def _():
            left[...] = own_ref[...].T

        @pl.when(home_ref[0] == 0)
        def _():
            left[...] = passed_ref[...].T

    ids = jnp.where(home_ref[0] == 1, ids_ref[...], sent_ref[...])
    ids_out[...] = ids
    heads, rel, query = make_query(ids[0:1], ids[1:2], left[...], table_ref[...])
    make_gradients(span, ids[2:3], ids[3:4], heads, rel, query, right[...], outs)


def gradient_shapes(features, edges):
    return [jax.ShapeDtypeStruct((features, edges), bf16)] * 4


def gradient_specs(features, span):
    return [across(features, span)] * 4


def cost(units, span, features, rows):
    return pl.CostEstimate(flops=1 << 40, bytes_accessed=1 << 32, transcendentals=0)


def query_call(ids, own, relation, rel_rows, width):
    edges = ids.shape[1]
    rows, features = own.shape
    return pl.pallas_call(
        query_kernel,
        grid=(edges // width,),
        in_specs=[across(4, width), whole(own.shape), whole(relation.shape)],
        out_specs=[across(features, width)] * 3 + [whole((2 * features, rel_rows))],
        out_shape=[
            jax.ShapeDtypeStruct((features, edges), bf16),
            jax.ShapeDtypeStruct((features, edges), f32),
            jax.ShapeDtypeStruct((features, edges), bf16),
            jax.ShapeDtypeStruct((2 * features, rel_rows), bf16),
        ],
        scratch_shapes=[pltpu.VMEM((features, rows), bf16), pltpu.VMEM((rel_rows, features), f32)],
        compiler_params=params(),
        cost_estimate=cost(2, edges, features, rows),
        name="queries",
    )(ids, own, relation)


def gradient_call(ids, heads, rel, query, partner, span, width):
    features, edges = heads.shape
    rows = partner.shape[0]
    return pl.pallas_call(
        functools.partial(gradient_kernel, span),
        grid=(edges // width,),
        in_specs=[across(4, width)] + [across(features, width)] * 3 + [whole(partner.shape)],
        out_specs=gradient_specs(features, width),
        out_shape=gradient_shapes(features, edges),
        scratch_shapes=[pltpu.VMEM((features, rows), bf16)],
        compiler_params=params(),
        cost_estimate=cost(3, edges, features, rows),
        name="gradients",
    )(ids, heads, rel, query, partner)


def paired_call(home, ids, sent_ids, own, met, passed, table, span, width):
    edges = ids.shape[1]
    rows, features = own.shape
    return pl.pallas_call(
        functools.partial(paired_kernel, span),
        grid=(edges // width,),
        in_specs=[pl.BlockSpec(memory_space=pltpu.SMEM), across(4, width), across(4, width)]
        + [whole(own.shape)] * 3
        + [whole(table.shape)],
        out_specs=gradient_specs(features, width) + [across(4, width)],
        out_shape=gradient_shapes(features, edges) + [jax.ShapeDtypeStruct(ids.shape, jnp.int32)],
        scratch_shapes=[pltpu.VMEM((features, rows), bf16)] * 2,
        compiler_params=params(),
        cost_estimate=cost(5, edges, features, rows),
        name="paired",
    )(home, ids, sent_ids, own, met, passed, table)


def scatter_kernel(chunk, lines, n_starts, *refs):
    first = pl.program_id(0) * chunk
    n_pairs = len(lines)
    ins = 2 * n_pairs + n_starts
    total = None
    for k, line in enumerate(lines):
        part = dot_nt(one_hot(refs[2 * k][line : line + 1, :], chunk, first), refs[2 * k + 1][...])
        total = part if total is None else total + part
    for start in refs[2 * n_pairs : ins]:
        total = total + start[...].astype(f32)
    for out_ref in refs[ins:]:
        out_ref[...] = total.astype(out_ref.dtype)


def scatter_call(pairs, rows, dtypes, starts=(), chunk=1024):
    features = pairs[0][2].shape[0]
    chunk = min(chunk, rows)
    operands, specs = [], []
    for ids, _, vectors in pairs:
        operands += [ids, vectors]
        specs += [whole(ids.shape), whole(vectors.shape)]
    down = pl.BlockSpec((chunk, features), lambda s: (s, 0))
    for start in starts:
        operands.append(start)
        specs.append(down)

    def kernel(*refs):
        scatter_kernel(chunk, [line for _, line, _ in pairs], len(starts), *refs)

    outs = pl.pallas_call(
        kernel,
        grid=(rows // chunk,),
        in_specs=specs,
        out_specs=[down] * len(dtypes),
        out_shape=[jax.ShapeDtypeStruct((rows, features), dtype) for dtype in dtypes],
        compiler_params=params(),
        cost_estimate=cost(1, sum(v.shape[1] for _, _, v in pairs), features, rows),
        name="scatter",
    )(*operands)
    return outs[0] if len(outs) == 1 else outs


def adagrad(grad, acc):
    rows, features = grad.shape
    mean = jnp.mean(grad * grad, axis=1, keepdims=True)
    acc_new = jnp.broadcast_to(acc, (128, rows)).T + mean
    scale = learn_rate / jnp.sqrt(acc_new)
    steps = [grad[:, k : k + 128] * scale for k in range(0, features, 128)]
    return acc_new.T[:1], jnp.concatenate(steps, axis=1)


def update_kernel(home_ref, entity_ref, acc_ref, local_ref, outer_ref, inner_ref, back_ref, new_ref, acc_new_ref):
    grad = local_ref[...] + outer_ref[...].astype(f32) + back_ref[...].astype(f32)
    grad = grad + jnp.where(home_ref[0] == 1, inner_ref[...].astype(f32), 0.0)
    acc_new, step = adagrad(grad, acc_ref[...])
    acc_new_ref[...] = acc_new
    new_ref[...] = (entity_ref[...].astype(f32) - step).astype(bf16)


def update_call(home, entity, acc, local, outer, inner, back, chunk=1024):
    rows, features = entity.shape
    down = pl.BlockSpec((chunk, features), lambda s: (s, 0))
    line = pl.BlockSpec((1, chunk), lambda s: (0, s))
    new, acc_new = pl.pallas_call(
        update_kernel,
        grid=(rows // chunk,),
        in_specs=[pl.BlockSpec(memory_space=pltpu.SMEM), down, line, down, down, down, down],
        out_specs=[down, line],
        out_shape=[jax.ShapeDtypeStruct((rows, features), bf16), jax.ShapeDtypeStruct((1, rows), f32)],
        compiler_params=params(),
        cost_estimate=cost(1, rows, features, rows),
        name="update",
    )(home, entity, acc.reshape(1, rows), local, outer, inner, back)
    return new, acc_new.reshape(rows)


def relation_kernel(relation_ref, acc_ref, total_ref, new_ref, acc_new_ref):
    n_rel = relation_ref.shape[0]
    total = total_ref[...].astype(f32)
    acc_new, step = adagrad(total, acc_ref[...])
    acc_new_ref[...] = acc_new[:, :n_rel]
    new_ref[...] = relation_ref[...] - step[:n_rel]


def relation_call(relation, acc, total):
    n_rel = relation.shape[0]
    line = jnp.pad(acc.reshape(1, n_rel), ((0, 0), (0, total.shape[0] - n_rel)), constant_values=1.0)
    new, acc_new = pl.pallas_call(
        relation_kernel,
        in_specs=[pl.BlockSpec(memory_space=pltpu.VMEM)] * 3,
        out_specs=[pl.BlockSpec(memory_space=pltpu.VMEM)] * 2,
        out_shape=[jax.ShapeDtypeStruct(relation.shape, f32), jax.ShapeDtypeStruct((1, n_rel), f32)],
        compiler_params=pltpu.CompilerParams(vmem_limit_bytes=VMEM_LIMIT),
        cost_estimate=cost(1, 1, 1, 1),
        name="relation",
    )(relation, line, total)
    return new, acc_new.reshape(n_rel)


def shares_kernel(pieces_ref, out_ref):
    share = jnp.sum(pieces_ref[...].astype(f32), axis=0).astype(bf16)
    for k in range(out_ref.shape[0]):
        out_ref[k] = share


def shares_call(pieces, copies):
    return pl.pallas_call(
        shares_kernel,
        in_specs=[pl.BlockSpec(memory_space=pltpu.VMEM)],
        out_specs=pl.BlockSpec(memory_space=pltpu.VMEM),
        out_shape=jax.ShapeDtypeStruct((copies,) + pieces.shape[1:], bf16),
        cost_estimate=cost(1, 1, 1, 1),
        name="shares",
    )(pieces)


def body(entity, entity_acc, relation, rel_acc, edge_src, edge_rel, edge_dst, negatives):
    axes = ("grp", "dom")
    groups, doms = lax.axis_size("grp"), lax.axis_size("dom")
    half = doms // 2
    rows, features = entity.shape
    n_rel = relation.shape[0]
    spans, span = negatives.shape[2:]
    edges = spans * span
    width = span * (2 - spans % 2)
    step = max(128, 8 * groups * doms)
    rel_rows = -(-n_rel // step) * step

    places = [(g, d) for g in range(groups) for d in range(doms)]

    def is_home(g, d):
        return g % 2 == d // half

    def send(block, to, only=lambda g, d: True):
        route = []
        for g, d in places:
            if only(g, d):
                h, e = to(g, d)
                route.append((g * doms + d, h % groups * doms + e % doms))
        return lax.ppermute(block, axes, route)

    def guest(g, d):
        return not is_home(g, d)

    def meeting(g, d):
        return (g ^ 1, d) if is_home(g, d) else (g, d + half)

    def parting(g, d):
        return (g, d + half) if is_home(g, d) else (g ^ 1, d)

    def neighbour(g, d):
        return g ^ 1, d

    home = (lax.axis_index("grp") % 2 == lax.axis_index("dom") // half).astype(jnp.int32).reshape(1)

    ids_one, ids_two = lines_call(edge_src, edge_rel, edge_dst, negatives.transpose(0, 2, 1, 3))
    met = send(entity, meeting)
    outer = send(entity, lambda g, d: (g + 1, d))
    heads, rel, query, table = query_call(ids_two, entity, relation, rel_rows, width)
    dl_two, dt_two, dc_two, dp_two = gradient_call(ids_two, heads, rel, query, outer, span, width)
    met, ids_one, dt_two = lax.optimization_barrier((met, ids_one, dt_two))
    passed = send(met, neighbour, is_home)
    sent_ids = send(ids_one, lambda g, d: (g ^ 1, d + half), guest)
    rel_part = scatter_call([(ids_two, 1, dp_two)], rel_rows, [f32])
    passed, sent_ids, rel_part = lax.optimization_barrier((passed, sent_ids, rel_part))
    dl_one, dt_one, dc_one, dp_one, ids_one = paired_call(
        home, ids_one, sent_ids, entity, met, passed, table, span, width
    )

    left_one = scatter_call([(ids_one, 0, dl_one)], rows, [bf16])
    guest_left = send(left_one, neighbour, guest)
    d_right_one = scatter_call([(ids_one, 2, dt_one), (ids_one, 3, dc_one)], rows, [bf16], [guest_left])
    back = send(d_right_one, parting)
    d_right_one, dp_one, dt_two, dl_two = lax.optimization_barrier((d_right_one, dp_one, dt_two, dl_two))

    planes = [[g * doms + q + x for g in range(groups) for x in range(2)] for q in range(0, doms, 2)]
    stacks = [[g * doms + q + x for q in range(0, doms, 2)] for g in range(groups) for x in range(2)]

    def exchange(pieces, sets):
        return lax.all_to_all(pieces, axes, 0, 0, axis_index_groups=sets, tiled=True)

    rel_sum = scatter_call([(ids_one, 1, dp_one)], rel_rows, [bf16], [rel_part])
    shares = exchange(rel_sum.reshape(2 * groups, -1, features), planes)
    rel_sum, dt_two = lax.optimization_barrier((rel_sum, dt_two))
    d_right_two = scatter_call([(ids_two, 2, dt_two), (ids_two, 3, dc_two)], rows, [bf16])
    back_outer = send(d_right_two, lambda g, d: (g - 1, d))
    shares, d_right_two = lax.optimization_barrier((shares, d_right_two))
    shares = exchange(shares_call(shares, len(stacks[0])), stacks)
    d_right_two, dl_two = lax.optimization_barrier((d_right_two, dl_two))
    local = scatter_call([(ids_two, 0, dl_two)], rows, [f32])
    shares, local = lax.optimization_barrier((shares, local))
    total = exchange(shares_call(shares, len(planes[0])), planes).reshape(rel_rows, features)
    entity_new, entity_acc_new = update_call(home, entity, entity_acc, local, back_outer, left_one, back)
    relation_new, rel_acc_new = relation_call(relation, rel_acc, total)
    return (entity_new, entity_acc_new, relation_new, rel_acc_new)


def solution(mesh):
    return jax.shard_map(
        body,
        mesh=mesh,
        in_specs=(
            P(("grp", "dom"), None),
            P(("grp", "dom")),
            P(),
            P(),
            P(("grp", "dom"), None, None),
            P(("grp", "dom"), None, None),
            P(("grp", "dom"), None, None),
            P(("grp", "dom"), None, None, None),
        ),
        out_specs=(P(("grp", "dom"), None), P(("grp", "dom")), P(), P()),
        check_vma=False,
    )
```

```python
import functools

import jax
import jax.numpy as jnp
from jax import lax
from jax.experimental import pallas as pl
from jax.experimental.pallas import tpu as pltpu
from jax.sharding import PartitionSpec as P

learn_rate = 0.3
bf16 = jnp.bfloat16
f32 = jnp.float32
VMEM_LIMIT = 52 << 20


def dot_nn(a, b):
    return jnp.dot(a, b, preferred_element_type=f32)


def dot_nt(a, b):
    return lax.dot_general(a, b, (((1,), (1,)), ((), ())), preferred_element_type=f32)


def one_hot(ids, rows, first=0):
    shape = (rows, ids.shape[1])
    match = (ids - first).astype(jnp.int16) == lax.broadcasted_iota(jnp.int16, shape, 0)
    return jnp.where(match, jnp.ones((), bf16), jnp.zeros((), bf16))


def whole(shape):
    return pl.BlockSpec(shape, lambda s: (0,) * len(shape))


def across(height, width):
    return pl.BlockSpec((height, width), lambda s: (0, s))


def params():
    return pltpu.CompilerParams(dimension_semantics=("arbitrary",), vmem_limit_bytes=VMEM_LIMIT)


def halves(a):
    middle = a.shape[0] // 2
    return a[:middle], a[middle:]


def make_query(source, rel_ids, left, rel_table):
    features, rows = left.shape
    heads = dot_nn(left, one_hot(source, rows))
    both = dot_nn(rel_table, one_hot(rel_ids, rel_table.shape[1]))
    rel = both[:features] + both[features:]
    h_re, h_im = halves(heads)
    r_re, r_im = halves(rel)
    query = jnp.concatenate([h_re * r_re - h_im * r_im, h_re * r_im + h_im * r_re], 0)
    return heads, rel, query.astype(bf16)


def make_gradients(span, targets, negatives, heads, rel, query, right, outs):
    width = query.shape[1]
    rows = right.shape[1]
    picked = dot_nn(right, one_hot(jnp.concatenate([targets, negatives], axis=1), rows))
    for first in range(0, width, span):
        part = slice(first, first + span)
        tails = picked[:, part]
        cands = picked[:, width + first : width + first + span].astype(bf16)
        span_gradients(tails, cands, heads[:, part], rel[:, part], query[:, part], [o.at[:, part] for o in outs])


def span_gradients(tails, cands, heads, rel, query, outs):
    heads_out, tails_out, cands_out, rels_out = outs
    query32 = query.astype(f32)
    positive = jnp.sum(query32 * tails, axis=0, keepdims=True)
    scores = dot_nn(cands.T, query)
    peak = jnp.maximum(jnp.max(scores, axis=0, keepdims=True), positive)
    expd = jnp.exp(scores - peak)
    own = jnp.exp(positive - peak)
    inverse = 1.0 / (own + jnp.sum(expd, axis=0, keepdims=True))
    shares = (expd * inverse).astype(bf16)
    coefficient = own * inverse - 1.0
    tails_out[...] = (coefficient * query32).astype(bf16)
    cands_out[...] = dot_nt(query, shares).astype(bf16)
    grad = coefficient * tails + dot_nn(cands, shares)
    g_re, g_im = halves(grad)
    r_re, r_im = halves(rel)
    h_re, h_im = halves(heads)
    heads_out[...] = jnp.concatenate(
        [g_re * r_re + g_im * r_im, g_im * r_re - g_re * r_im], 0
    ).astype(bf16)
    rels_out[...] = jnp.concatenate(
        [g_re * h_re + g_im * h_im, g_im * h_re - g_re * h_im], 0
    ).astype(bf16)


def lines_kernel(source_ref, rel_ref, target_ref, negatives_ref, *outs):
    _, spans, _, span = negatives_ref.shape
    for bucket, out_ref in enumerate(outs):
        for line, ref in enumerate((source_ref, rel_ref, target_ref)):
            out_ref[line : line + 1] = ref[0, bucket : bucket + 1]
        for s in range(spans):
            out_ref[3:4, s * span : (s + 1) * span] = negatives_ref[0, s, bucket : bucket + 1]


def lines_call(*arrays):
    edges = arrays[0].shape[2]
    return pl.pallas_call(
        lines_kernel,
        in_specs=[pl.BlockSpec(memory_space=pltpu.VMEM)] * 4,
        out_specs=[pl.BlockSpec(memory_space=pltpu.VMEM)] * 2,
        out_shape=[jax.ShapeDtypeStruct((4, edges), jnp.int32)] * 2,
        cost_estimate=cost(1, 1, 1, 1),
        name="lines",
    )(*arrays)


def query_kernel(ids_ref, own_ref, relation_ref, heads_ref, rel_ref, query_ref, table_ref, left, padded):
    @pl.when(pl.program_id(0) == 0)
    def _():
        n_rel, features = relation_ref.shape
        left[...] = own_ref[...].T
        padded[:n_rel] = relation_ref[...]
        padded[n_rel:] = jnp.zeros((padded.shape[0] - n_rel, features), f32)
        across_rel = padded[...].T
        high = across_rel.astype(bf16)
        table_ref[:features] = high
        table_ref[features:] = (across_rel - high.astype(f32)).astype(bf16)

    ids = ids_ref[...]
    heads, rel, query = make_query(ids[0:1], ids[1:2], left[...], table_ref[...])
    heads_ref[...] = heads.astype(bf16)
    rel_ref[...] = rel
    query_ref[...] = query


def gradient_kernel(span, ids_ref, heads_ref, rel_ref, query_ref, partner_ref, *rest):
    *outs, right = rest

    @pl.when(pl.program_id(0) == 0)
    def _():
        right[...] = partner_ref[...].T

    ids = ids_ref[...]
    heads = heads_ref[...].astype(f32)
    make_gradients(span, ids[2:3], ids[3:4], heads, rel_ref[...], query_ref[...], right[...], outs)


def paired_kernel(span, home_ref, ids_ref, sent_ref, own_ref, met_ref, passed_ref, table_ref, *rest):
    *outs, ids_out, left, right = rest

    @pl.when(pl.program_id(0) == 0)
    def _():
        right[...] = met_ref[...].T

        @pl.when(home_ref[0] == 1)
        def _():
            left[...] = own_ref[...].T

        @pl.when(home_ref[0] == 0)
        def _():
            left[...] = passed_ref[...].T

    ids = jnp.where(home_ref[0] == 1, ids_ref[...], sent_ref[...])
    ids_out[...] = ids
    heads, rel, query = make_query(ids[0:1], ids[1:2], left[...], table_ref[...])
    make_gradients(span, ids[2:3], ids[3:4], heads, rel, query, right[...], outs)


def gradient_shapes(features, edges):
    return [jax.ShapeDtypeStruct((features, edges), bf16)] * 4


def gradient_specs(features, span):
    return [across(features, span)] * 4


def cost(units, span, features, rows):
    return pl.CostEstimate(flops=1 << 40, bytes_accessed=1 << 32, transcendentals=0)


def query_call(ids, own, relation, rel_rows, width):
    edges = ids.shape[1]
    rows, features = own.shape
    return pl.pallas_call(
        query_kernel,
        grid=(edges // width,),
        in_specs=[across(4, width), whole(own.shape), whole(relation.shape)],
        out_specs=[across(features, width)] * 3 + [whole((2 * features, rel_rows))],
        out_shape=[
            jax.ShapeDtypeStruct((features, edges), bf16),
            jax.ShapeDtypeStruct((features, edges), f32),
            jax.ShapeDtypeStruct((features, edges), bf16),
            jax.ShapeDtypeStruct((2 * features, rel_rows), bf16),
        ],
        scratch_shapes=[pltpu.VMEM((features, rows), bf16), pltpu.VMEM((rel_rows, features), f32)],
        compiler_params=params(),
        cost_estimate=cost(2, edges, features, rows),
        name="queries",
    )(ids, own, relation)


def gradient_call(ids, heads, rel, query, partner, span, width):
    features, edges = heads.shape
    rows = partner.shape[0]
    return pl.pallas_call(
        functools.partial(gradient_kernel, span),
        grid=(edges // width,),
        in_specs=[across(4, width)] + [across(features, width)] * 3 + [whole(partner.shape)],
        out_specs=gradient_specs(features, width),
        out_shape=gradient_shapes(features, edges),
        scratch_shapes=[pltpu.VMEM((features, rows), bf16)],
        compiler_params=params(),
        cost_estimate=cost(3, edges, features, rows),
        name="gradients",
    )(ids, heads, rel, query, partner)


def paired_call(home, ids, sent_ids, own, met, passed, table, span, width):
    edges = ids.shape[1]
    rows, features = own.shape
    return pl.pallas_call(
        functools.partial(paired_kernel, span),
        grid=(edges // width,),
        in_specs=[pl.BlockSpec(memory_space=pltpu.SMEM), across(4, width), across(4, width)]
        + [whole(own.shape)] * 3
        + [whole(table.shape)],
        out_specs=gradient_specs(features, width) + [across(4, width)],
        out_shape=gradient_shapes(features, edges) + [jax.ShapeDtypeStruct(ids.shape, jnp.int32)],
        scratch_shapes=[pltpu.VMEM((features, rows), bf16)] * 2,
        compiler_params=params(),
        cost_estimate=cost(5, edges, features, rows),
        name="paired",
    )(home, ids, sent_ids, own, met, passed, table)


def scatter_kernel(chunk, lines, n_starts, *refs):
    first = pl.program_id(0) * chunk
    n_pairs = len(lines)
    ins = 2 * n_pairs + n_starts
    total = None
    for k, line in enumerate(lines):
        part = dot_nt(one_hot(refs[2 * k][line : line + 1, :], chunk, first), refs[2 * k + 1][...])
        total = part if total is None else total + part
    for start in refs[2 * n_pairs : ins]:
        total = total + start[...].astype(f32)
    for out_ref in refs[ins:]:
        out_ref[...] = total.astype(out_ref.dtype)


def scatter_call(pairs, rows, dtypes, starts=(), chunk=1024):
    features = pairs[0][2].shape[0]
    chunk = min(chunk, rows)
    operands, specs = [], []
    for ids, _, vectors in pairs:
        operands += [ids, vectors]
        specs += [whole(ids.shape), whole(vectors.shape)]
    down = pl.BlockSpec((chunk, features), lambda s: (s, 0))
    for start in starts:
        operands.append(start)
        specs.append(down)

    def kernel(*refs):
        scatter_kernel(chunk, [line for _, line, _ in pairs], len(starts), *refs)

    outs = pl.pallas_call(
        kernel,
        grid=(rows // chunk,),
        in_specs=specs,
        out_specs=[down] * len(dtypes),
        out_shape=[jax.ShapeDtypeStruct((rows, features), dtype) for dtype in dtypes],
        compiler_params=params(),
        cost_estimate=cost(1, sum(v.shape[1] for _, _, v in pairs), features, rows),
        name="scatter",
    )(*operands)
    return outs[0] if len(outs) == 1 else outs


def adagrad(grad, acc):
    rows, features = grad.shape
    mean = jnp.mean(grad * grad, axis=1, keepdims=True)
    acc_new = jnp.broadcast_to(acc, (128, rows)).T + mean
    scale = learn_rate / jnp.sqrt(acc_new)
    steps = [grad[:, k : k + 128] * scale for k in range(0, features, 128)]
    return acc_new.T[:1], jnp.concatenate(steps, axis=1)


def update_kernel(home_ref, entity_ref, acc_ref, local_ref, outer_ref, inner_ref, back_ref, new_ref, acc_new_ref):
    grad = local_ref[...] + outer_ref[...].astype(f32) + back_ref[...].astype(f32)
    grad = grad + jnp.where(home_ref[0] == 1, inner_ref[...].astype(f32), 0.0)
    acc_new, step = adagrad(grad, acc_ref[...])
    acc_new_ref[...] = acc_new
    new_ref[...] = (entity_ref[...].astype(f32) - step).astype(bf16)


def update_call(home, entity, acc, local, outer, inner, back, chunk=1024):
    rows, features = entity.shape
    down = pl.BlockSpec((chunk, features), lambda s: (s, 0))
    line = pl.BlockSpec((1, chunk), lambda s: (0, s))
    new, acc_new = pl.pallas_call(
        update_kernel,
        grid=(rows // chunk,),
        in_specs=[pl.BlockSpec(memory_space=pltpu.SMEM), down, line, down, down, down, down],
        out_specs=[down, line],
        out_shape=[jax.ShapeDtypeStruct((rows, features), bf16), jax.ShapeDtypeStruct((1, rows), f32)],
        compiler_params=params(),
        cost_estimate=cost(1, rows, features, rows),
        name="update",
    )(home, entity, acc.reshape(1, rows), local, outer, inner, back)
    return new, acc_new.reshape(rows)


def relation_kernel(relation_ref, acc_ref, total_ref, new_ref, acc_new_ref):
    n_rel = relation_ref.shape[0]
    total = total_ref[...].astype(f32)
    acc_new, step = adagrad(total, acc_ref[...])
    acc_new_ref[...] = acc_new[:, :n_rel]
    new_ref[...] = relation_ref[...] - step[:n_rel]


def relation_call(relation, acc, total):
    n_rel = relation.shape[0]
    line = jnp.pad(acc.reshape(1, n_rel), ((0, 0), (0, total.shape[0] - n_rel)), constant_values=1.0)
    new, acc_new = pl.pallas_call(
        relation_kernel,
        in_specs=[pl.BlockSpec(memory_space=pltpu.VMEM)] * 3,
        out_specs=[pl.BlockSpec(memory_space=pltpu.VMEM)] * 2,
        out_shape=[jax.ShapeDtypeStruct(relation.shape, f32), jax.ShapeDtypeStruct((1, n_rel), f32)],
        compiler_params=pltpu.CompilerParams(vmem_limit_bytes=VMEM_LIMIT),
        cost_estimate=cost(1, 1, 1, 1),
        name="relation",
    )(relation, line, total)
    return new, acc_new.reshape(n_rel)


def shares_kernel(pieces_ref, out_ref):
    share = jnp.sum(pieces_ref[...].astype(f32), axis=0).astype(bf16)
    for k in range(out_ref.shape[0]):
        out_ref[k] = share


def shares_call(pieces, copies):
    return pl.pallas_call(
        shares_kernel,
        in_specs=[pl.BlockSpec(memory_space=pltpu.VMEM)],
        out_specs=pl.BlockSpec(memory_space=pltpu.VMEM),
        out_shape=jax.ShapeDtypeStruct((copies,) + pieces.shape[1:], bf16),
        cost_estimate=cost(1, 1, 1, 1),
        name="shares",
    )(pieces)


def body(entity, entity_acc, relation, rel_acc, edge_src, edge_rel, edge_dst, negatives):
    axes = ("grp", "dom")
    groups, doms = lax.axis_size("grp"), lax.axis_size("dom")
    half = doms // 2
    rows, features = entity.shape
    n_rel = relation.shape[0]
    spans, span = negatives.shape[2:]
    edges = spans * span
    width = span * (2 - spans % 2)
    step = max(128, 8 * groups * doms)
    rel_rows = -(-n_rel // step) * step

    places = [(g, d) for g in range(groups) for d in range(doms)]

    def is_home(g, d):
        return g % 2 == d // half

    def send(block, to, only=lambda g, d: True):
        route = []
        for g, d in places:
            if only(g, d):
                h, e = to(g, d)
                route.append((g * doms + d, h % groups * doms + e % doms))
        return lax.ppermute(block, axes, route)

    def guest(g, d):
        return not is_home(g, d)

    def meeting(g, d):
        return (g ^ 1, d) if is_home(g, d) else (g, d + half)

    def parting(g, d):
        return (g, d + half) if is_home(g, d) else (g ^ 1, d)

    def neighbour(g, d):
        return g ^ 1, d

    home = (lax.axis_index("grp") % 2 == lax.axis_index("dom") // half).astype(jnp.int32).reshape(1)

    ids_one, ids_two = lines_call(edge_src, edge_rel, edge_dst, negatives.transpose(0, 2, 1, 3))
    met = send(entity, meeting)
    outer = send(entity, lambda g, d: (g + 1, d))
    heads, rel, query, table = query_call(ids_two, entity, relation, rel_rows, width)
    dl_two, dt_two, dc_two, dp_two = gradient_call(ids_two, heads, rel, query, outer, span, width)
    met, ids_one, dt_two = lax.optimization_barrier((met, ids_one, dt_two))
    passed = send(met, neighbour, is_home)
    sent_ids = send(ids_one, lambda g, d: (g ^ 1, d + half), guest)
    rel_part = scatter_call([(ids_two, 1, dp_two)], rel_rows, [f32])
    passed, sent_ids, rel_part = lax.optimization_barrier((passed, sent_ids, rel_part))
    dl_one, dt_one, dc_one, dp_one, ids_one = paired_call(
        home, ids_one, sent_ids, entity, met, passed, table, span, width
    )

    left_one = scatter_call([(ids_one, 0, dl_one)], rows, [bf16])
    guest_left = send(left_one, neighbour, guest)
    left_one, dp_one = lax.optimization_barrier((left_one, dp_one))
    rel_sum = scatter_call([(ids_one, 1, dp_one)], rel_rows, [bf16], [rel_part])
    rel_sum, dt_one = lax.optimization_barrier((rel_sum, dt_one))
    d_right_one = scatter_call([(ids_one, 2, dt_one), (ids_one, 3, dc_one)], rows, [bf16], [guest_left])
    back = send(d_right_one, parting)
    d_right_one, rel_sum, dt_two, dl_two = lax.optimization_barrier((d_right_one, rel_sum, dt_two, dl_two))

    planes = [[g * doms + q + x for g in range(groups) for x in range(2)] for q in range(0, doms, 2)]
    stacks = [[g * doms + q + x for q in range(0, doms, 2)] for g in range(groups) for x in range(2)]

    def exchange(pieces, sets):
        return lax.all_to_all(pieces, axes, 0, 0, axis_index_groups=sets, tiled=True)

    shares = exchange(rel_sum.reshape(2 * groups, -1, features), planes)
    d_right_two = scatter_call([(ids_two, 2, dt_two), (ids_two, 3, dc_two)], rows, [bf16])
    back_outer = send(d_right_two, lambda g, d: (g - 1, d))
    shares, d_right_two = lax.optimization_barrier((shares, d_right_two))
    shares = exchange(shares_call(shares, len(stacks[0])), stacks)
    d_right_two, dl_two = lax.optimization_barrier((d_right_two, dl_two))
    local = scatter_call([(ids_two, 0, dl_two)], rows, [f32])
    shares, local = lax.optimization_barrier((shares, local))
    total = exchange(shares_call(shares, len(planes[0])), planes).reshape(rel_rows, features)
    entity_new, entity_acc_new = update_call(home, entity, entity_acc, local, back_outer, left_one, back)
    relation_new, rel_acc_new = relation_call(relation, rel_acc, total)
    return (entity_new, entity_acc_new, relation_new, rel_acc_new)


def solution(mesh):
    return jax.shard_map(
        body,
        mesh=mesh,
        in_specs=(
            P(("grp", "dom"), None),
            P(("grp", "dom")),
            P(),
            P(),
            P(("grp", "dom"), None, None),
            P(("grp", "dom"), None, None),
            P(("grp", "dom"), None, None),
            P(("grp", "dom"), None, None, None),
        ),
        out_specs=(P(("grp", "dom"), None), P(("grp", "dom")), P(), P()),
        check_vma=False,
    )
```
